32 devices in a mesh: task: 4 (over x, core), tensor: 4 (over z), dp: 2 (over y).
Axes of the slice: x: 2, y: 2, z: 4, core: 2. Of those that a mesh axis runs over, the one named last changes fastest.
Arguments:
- hidden: bfloat16 [1024, 4608], P(('task', 'dp')), may hold values from -6 to 6
- pre_gain: float32 [4608], replicated, may hold values from 0.1 to 1.9
- base_query: bfloat16 [4608, 512], P('dp', 'tensor'), may hold values from -0.09375 to 0.09375
- base_keyval: bfloat16 [2, 4608, 256], P(None, 'dp', 'tensor'), may hold values from -0.09375 to 0.09375
- base_output: bfloat16 [512, 4608], P('tensor', 'dp'), may hold values from -0.25 to 0.25
- delta_query: bfloat16 [4, 4608, 512], P('task', 'dp', 'tensor'), may hold values from -0.046875 to 0.046875
- delta_keyval: bfloat16 [4, 2, 4608, 256], P('task', None, 'dp', 'tensor'), may hold values from -0.046875 to 0.046875
- delta_output: bfloat16 [4, 512, 4608], P('task', 'tensor', 'dp'), may hold values from -0.125 to 0.125
- trim_query: int32 [4, 72, 8], P('task', 'dp', 'tensor'), may hold values 0 or 1
- trim_keyval: int32 [4, 2, 72, 4], P('task', None, 'dp', 'tensor'), may hold values 0 or 1
- trim_output: int32 [4, 8, 72], P('task', 'tensor', 'dp'), may hold values 0 or 1
- sign_query: int32 [72, 8], P('dp', 'tensor'), may hold values from 0 to 1
- sign_keyval: int32 [2, 72, 4], P(None, 'dp', 'tensor'), may hold values from 0 to 1
- sign_output: int32 [8, 72], P('tensor', 'dp'), may hold values from 0 to 1
- post_gain: float32 [4608], replicated, may hold values from 0.1 to 1.9
- final_gain: float32 [4608], replicated, may hold values from 0.1 to 1.9
- unembedding: bfloat16 [28672, 4608], P(('task', 'tensor', 'dp')), may hold values from -0.375 to 0.375
- targets: int32 [1024], replicated, may hold values from 0 to 28671
- loss_mask: int32 [1024], replicated, may hold values 0 or 1
Outputs:
- token_loss: float32 [1024], P(('task', 'dp'))
- summary: float32 [2], replicated
The draws below stay inside these ranges and needn't reach their ends.
All inputs are finite; a program needn't handle non-finite values. No bound on the sum of `trim_query` or of `trim_keyval` or of `trim_output` on one device may be relied on, other than what follows from the above.
Results may differ from the reference program's by a relative error of at most 0.0045.
Values may be sent and summed in bfloat16 or wider, within the bound.
No kernel may reach another device: no remote copies, remote signals or barrier semaphores. Data moves between devices by JAX's collectives and lax.ppermute only.
A program may use at most 128 MiB of HBM per device.

```python
import jax
import jax.numpy as jnp
from jax import lax

D = 4608
HD = 128
BLK = 64
VOCAB_DEV = 896
H = 4
KVH = 2
VOCAB = 28672
LEN = 1024
TASKS = 4


def with_ends(array, key, least, largest):
    dims = array.shape
    spot = [jax.random.randint(jax.random.fold_in(key, axis), (), 0, dims[axis]) for axis in range(len(dims))]
    array = array.at[tuple(spot)].set(least)
    longest = dims.index(max(dims))
    spot[longest] = (spot[longest] + 1) % dims[longest]
    return array.at[tuple(spot)].set(largest)


def block_levels(rng, dims, split, low, high):
    factor_of, own = 1.0, jax.random.fold_in(rng, 6)
    for axis_at, blocks in split:
        draws = jnp.exp(jax.random.uniform(jax.random.fold_in(own, axis_at), (blocks,), jnp.float32, low / len(split), high / len(split)))
        factor_of = factor_of * jnp.repeat(draws, dims[axis_at] // blocks).reshape([-1 if axis == axis_at else 1 for axis in range(len(dims))])
    return factor_of


def noise(own_key, extent, deviation, bound, pieces=(), kind=jnp.bfloat16):
    values = deviation * jax.random.normal(own_key, extent, jnp.float32)
    if pieces:
        values = values * block_levels(own_key, extent, pieces, -0.22, 0.18)
    return jnp.clip(values, -bound, bound).astype(kind)


def setup_inputs(seed: int = 0) -> dict:
    key_list = jax.random.split(jax.random.key(seed), 20)
    hidden = noise(key_list[0], (LEN, D), 1.0, 6.0, ((0, 8),))
    pre_gain = jnp.clip(1.0 + 0.18 * jax.random.normal(key_list[1], (D,), jnp.float32), 0.1, 1.9)
    base_query = noise(key_list[2], (D, H * HD), D ** -0.5, 0.09375, ((0, 2), (1, 4)))
    base_keyval = noise(key_list[3], (2, D, KVH * HD), D ** -0.5, 0.09375, ((1, 2), (2, 4)))
    base_output = noise(key_list[4], (H * HD, D), (H * HD) ** -0.5, 0.25, ((0, 4), (1, 2)))
    delta_query = noise(key_list[5], (TASKS, D, H * HD), (4 * D) ** -0.5, 0.046875, ((0, 4), (1, 2), (2, 4)))
    delta_keyval = noise(key_list[6], (TASKS, 2, D, KVH * HD), (4 * D) ** -0.5, 0.046875, ((0, 4), (2, 2), (3, 4)))
    delta_output = noise(key_list[7], (TASKS, H * HD, D), (4 * H * HD) ** -0.5, 0.125, ((0, 4), (1, 4), (2, 2)))
    trim_query = with_ends((jax.random.randint(key_list[8], (TASKS, D // BLK, H * HD // BLK), 0, 4) < 3).astype(jnp.int32), jax.random.fold_in(key_list[8], 1), 0, 1)
    trim_keyval = with_ends((jax.random.randint(key_list[9], (TASKS, 2, D // BLK, KVH * HD // BLK), 0, 4) < 3).astype(jnp.int32), jax.random.fold_in(key_list[9], 1), 0, 1)
    trim_output = with_ends((jax.random.randint(key_list[10], (TASKS, H * HD // BLK, D // BLK), 0, 4) < 3).astype(jnp.int32), jax.random.fold_in(key_list[10], 1), 0, 1)
    sign_query = with_ends(jax.random.randint(key_list[11], (D // BLK, H * HD // BLK), 0, 2), jax.random.fold_in(key_list[11], 1), 0, 1).astype(jnp.int32)
    sign_keyval = with_ends(jax.random.randint(key_list[12], (2, D // BLK, KVH * HD // BLK), 0, 2), jax.random.fold_in(key_list[12], 1), 0, 1).astype(jnp.int32)
    sign_output = with_ends(jax.random.randint(key_list[13], (H * HD // BLK, D // BLK), 0, 2), jax.random.fold_in(key_list[13], 1), 0, 1).astype(jnp.int32)
    post_gain = jnp.clip(1.0 + 0.18 * jax.random.normal(key_list[14], (D,), jnp.float32), 0.1, 1.9)
    final_gain = jnp.clip(1.0 + 0.18 * jax.random.normal(key_list[15], (D,), jnp.float32), 0.1, 1.9)
    unembedding = noise(key_list[16], (VOCAB, D), (D // 16) ** -0.5, 0.375, ((0, 32),))
    targets = with_ends(jax.random.randint(key_list[17], (LEN,), 0, VOCAB), jax.random.fold_in(key_list[17], 1), 0, VOCAB - 1).astype(jnp.int32)
    loss_mask = with_ends((jax.random.randint(key_list[18], (LEN,), 0, 4) < 3).astype(jnp.int32), jax.random.fold_in(key_list[18], 1), 0, 1)
    return {"hidden": hidden, "pre_gain": pre_gain, "base_query": base_query, "base_keyval": base_keyval, "base_output": base_output, "delta_query": delta_query, "delta_keyval": delta_keyval, "delta_output": delta_output, "trim_query": trim_query, "trim_keyval": trim_keyval, "trim_output": trim_output, "sign_query": sign_query, "sign_keyval": sign_keyval, "sign_output": sign_output, "post_gain": post_gain, "final_gain": final_gain, "unembedding": unembedding, "targets": targets, "loss_mask": loss_mask}


EPSILON = 1e-06
QUERY_SCALE = 1.0 / 12.0
ROPE_BASE = 10000.0
SCORE_CAP = 50.0
LOGIT_CAP = 30.0

def trim_delta(deltas, trim_bits, sign_bits):
    layout = deltas.shape
    row_blocks = layout[-2] // BLK
    col_blocks = layout[-1] // BLK
    blocks = deltas.reshape(layout[:-2] + (row_blocks, BLK, col_blocks, BLK))
    wanted = (2 * sign_bits - 1).astype(jnp.float32)[..., :, None, :, None]
    keeping = (trim_bits[..., :, None, :, None] == 1) & (jnp.sign(blocks.astype(jnp.float32)) == wanted)
    return jnp.where(keeping, blocks, jnp.zeros_like(blocks)).reshape(layout)

def merge_weights(base_part, deltas, trim_bits, sign_bits):
    kept_part = trim_delta(deltas, trim_bits, sign_bits)
    totals = lax.optimization_barrier(jnp.sum(kept_part.astype(jnp.float32), axis=0))
    counts = lax.optimization_barrier(jnp.sum((kept_part != 0).astype(jnp.float32), axis=0))
    return (base_part.astype(jnp.float32) + totals / jnp.maximum(counts, 1.0)).astype(jnp.bfloat16)

def rms_norm(values, gain):
    scale = lax.rsqrt(lax.optimization_barrier(jnp.mean(values * values, axis=-1, keepdims=True)) + EPSILON)
    return values * scale * gain

def rotate(values, angles):
    half_width = values.shape[-1] // 2
    first = values[..., :half_width]
    second = values[..., half_width:]
    cosine = jnp.cos(angles)
    sine = jnp.sin(angles)
    return jnp.concatenate([first * cosine - second * sine, second * cosine + first * sine], axis=-1)

def reference(hidden, pre_gain, base_query, base_keyval, base_output, delta_query, delta_keyval, delta_output, trim_query, trim_keyval, trim_output, sign_query, sign_keyval, sign_output, post_gain, final_gain, unembedding, targets, loss_mask):
    merged_query = merge_weights(base_query, delta_query, trim_query, sign_query)
    merged_keyval = merge_weights(base_keyval, delta_keyval, trim_keyval, sign_keyval)
    merged_output = merge_weights(base_output, delta_output, trim_output, sign_output)
    residual = hidden.astype(jnp.float32)
    normed = rms_norm(residual, pre_gain).astype(jnp.bfloat16)
    index_list = jnp.arange(LEN, dtype=jnp.int32)
    positions = index_list.astype(jnp.float32)
    frequencies = jnp.exp(-jnp.log(ROPE_BASE) * 2.0 * jnp.arange(HD // 2, dtype=jnp.int32).astype(jnp.float32) / HD)
    angles = (positions[:, None] * frequencies[None, :])[:, None, :]
    queries = jnp.dot(normed, merged_query, preferred_element_type=jnp.float32).reshape(LEN, H, HD)
    queries = (rotate(queries, angles) * QUERY_SCALE).astype(jnp.bfloat16)
    keys_all = jnp.dot(normed, merged_keyval[0], preferred_element_type=jnp.float32).reshape(LEN, KVH, HD)
    keys_all = rotate(keys_all, angles).astype(jnp.bfloat16)
    values_all = jnp.dot(normed, merged_keyval[1], preferred_element_type=jnp.float32).reshape(LEN, KVH, HD).astype(jnp.bfloat16)
    causal = index_list[:, None] >= index_list[None, :]

    def one_group(items):
        query_pair, key_head, value_head = items
        scores = jnp.einsum('hqd,kd->hqk', query_pair.astype(jnp.float32), key_head.astype(jnp.float32))
        capped = SCORE_CAP * jnp.tanh(scores / SCORE_CAP)
        weights = jnp.where(causal[None], jnp.exp(capped), 0.0)
        rounded = lax.optimization_barrier(weights.astype(jnp.bfloat16)).astype(jnp.float32)
        numerator = jnp.einsum('hqk,kd->hqd', rounded, value_head.astype(jnp.float32))
        denominator = lax.optimization_barrier(jnp.sum(weights, axis=-1))
        return (numerator / denominator[..., None]).astype(jnp.bfloat16)
    grouped = jnp.transpose(queries.reshape(LEN, KVH, 2, HD), (1, 2, 0, 3))
    outputs = lax.map(one_group, (grouped, jnp.transpose(keys_all, (1, 0, 2)), jnp.transpose(values_all, (1, 0, 2))))
    attention = jnp.transpose(outputs, (2, 0, 1, 3)).reshape(LEN, H * HD)
    projected = jnp.dot(attention, merged_output, preferred_element_type=jnp.float32)
    stream = residual + rms_norm(projected, post_gain)
    final = rms_norm(stream, final_gain).astype(jnp.bfloat16)
    block_rows = VOCAB_DEV * 8
    tables = unembedding.reshape(-1, block_rows, D)
    offsets = jnp.arange(tables.shape[0], dtype=jnp.int32) * block_rows

    def vocab_step(carried, items):
        table, offset = items
        logits = lax.dot_general(final, table, (((1,), (1,)), ((), ())), preferred_element_type=jnp.float32)
        capped = LOGIT_CAP * jnp.tanh(logits / LOGIT_CAP)
        vocab_ids = offset + jnp.arange(block_rows, dtype=jnp.int32)
        sumexp = carried[0] + lax.optimization_barrier(jnp.sum(jnp.exp(capped), axis=1))
        target_logit = carried[1] + lax.optimization_barrier(jnp.sum(jnp.where(targets[:, None] == vocab_ids[None, :], capped, 0.0), axis=1))
        return ((sumexp, target_logit), None)
    zeros = jnp.zeros((LEN,), jnp.float32)
    (sumexp, target_logit), _ = lax.scan(vocab_step, (zeros, zeros), (tables, offsets))
    counted = loss_mask.astype(jnp.float32)
    token_loss = (jnp.log(sumexp) - target_logit) * counted
    summary = jnp.stack([jnp.sum(token_loss), jnp.sum(counted)])
    return (token_loss, summary)
```

```python
import functools

import jax
import jax.numpy as jnp
from jax import lax
from jax.experimental import pallas as pl
from jax.experimental.pallas import tpu as pltpu
from jax.sharding import PartitionSpec as P

BLK = 64
LANES = 128

EPSILON = 1e-06
QUERY_SCALE = 1.0 / 12.0
ROPE_BASE = 10000.0
SCORE_CAP = 50.0
LOGIT_CAP = 30.0


VMEM = pl.BlockSpec(memory_space=pltpu.VMEM)
SMEM = pl.BlockSpec(memory_space=pltpu.SMEM)


def kernel_call(body, inputs, in_specs, outputs, scratch=(), flops=1, transcendentals=0, name=None):
    moved = sum(a.size * a.dtype.itemsize for a in inputs)
    moved += sum(int(jnp.dtype(o.dtype).itemsize) * o.size for o in outputs)
    return pl.pallas_call(
        body,
        out_shape=outputs,
        in_specs=in_specs,
        out_specs=[VMEM] * len(outputs),
        scratch_shapes=list(scratch),
        name=name,
        cost_estimate=pl.CostEstimate(
            flops=flops, bytes_accessed=moved, transcendentals=transcendentals
        ),
    )(*inputs)


def shape_of(dims, dtype):
    return jax.ShapeDtypeStruct(tuple(dims), dtype)


def swap(block, axis, mask):
    count = lax.axis_size(axis)
    return lax.ppermute(block, axis, [(i, i ^ mask) for i in range(count)])


def swap_two(block, task_mask, dp_mask):
    tasks, halves = lax.axis_size("task"), lax.axis_size("dp")
    route = []
    for t in range(tasks):
        for d in range(halves):
            route.append((t * halves + d, (t ^ task_mask) * halves + (d ^ dp_mask)))
    return lax.ppermute(block, ("task", "dp"), route)


def gather_group(block):
    tasks, halves = lax.axis_size("task"), lax.axis_size("dp")
    near = [(0, 0, block)]
    for tm in range(0, tasks, 2):
        for dm in range(halves):
            if tm or dm:
                if not dm:
                    got = swap(block, "task", tm)
                elif not tm:
                    got = swap(block, "dp", dm)
                else:
                    got = swap_two(block, tm, dm)
                near.append((tm, dm, got))
    return near + [(tm ^ 1, dm, swap(b, "task", 1)) for tm, dm, b in near]


def total_over(value, axis):
    count = lax.axis_size(axis)
    if count <= 4:
        parts = [swap(value, axis, m) for m in range(1, count)]
        for part in parts:
            value = value + part
        return value
    step = 1
    while step < count:
        value = value + swap(value, axis, step)
        step *= 2
    return value


def total_over_group(value):
    tasks, halves = lax.axis_size("task"), lax.axis_size("dp")
    parts = []
    for tm in range(0, tasks, 2):
        for dm in range(halves):
            if tm or dm:
                parts.append(swap_two(value, tm, dm))
    for part in parts:
        value = value + part
    return value + swap(value, "task", 1)


def block_code(trim, sign):
    return (trim * (2 * sign - 1)).astype(jnp.float32)


def transpose_columns(source, out_ref):
    for c in range(out_ref.shape[0] // LANES):
        out_ref[c * LANES : (c + 1) * LANES, :] = source(c).astype(jnp.float32).T


def keyval_tile(ref, c):
    both = ref[:, :, c * LANES : (c + 1) * LANES]
    return both.reshape(2 * both.shape[1], LANES)


def trim_input_body(tasks, place, tq, tkv, sq, skv, dq, dkv, *rest):
    outs, turned = rest[:-1], rest[-1]
    me = place[0]
    transpose_columns(lambda c: keyval_tile(dkv.at[0], c), turned)
    rows = outs[0].shape[0]
    blocks = rows // BLK
    low = lax.broadcasted_iota(jnp.int32, (BLK, LANES), 1) < BLK
    for j in range(tasks):
        first = (me ^ j) * blocks
        for r in range(blocks):
            b = first + r
            at = pl.ds(pl.multiple_of(b * BLK, BLK), BLK)
            here = slice(r * BLK, (r + 1) * BLK)
            code = jnp.where(
                low, block_code(tq[0, 0, b], sq[0, b]), block_code(tq[0, 1, b], sq[1, b])
            )
            d = dq[0, at, :].astype(jnp.float32)
            outs[j][here, :LANES] = jnp.where(d * code > 0, d, 0.0).astype(jnp.bfloat16)
            code = jnp.where(
                low, block_code(tkv[0, 0, 0, b], skv[0, 0, b]), block_code(tkv[0, 1, 0, b], skv[1, 0, b])
            )
            d = turned[at, :]
            outs[j][here, LANES:] = jnp.where(d * code > 0, d, 0.0).astype(jnp.bfloat16)


def trim_output_body(tasks, place, to, so, do, *outs):
    me = place[0]
    rows, width = outs[0].shape
    low = lax.broadcasted_iota(jnp.int32, (rows, LANES), 1) < BLK
    for j in range(tasks):
        first = (me ^ j) * rows
        at = pl.ds(pl.multiple_of(first, rows), rows)
        b = first // BLK
        for c in range(width // LANES):
            cols = slice(c * LANES, (c + 1) * LANES)
            code = jnp.where(
                low,
                block_code(to[0, b, 2 * c], so[b, 2 * c]),
                block_code(to[0, b, 2 * c + 1], so[b, 2 * c + 1]),
            )
            d = do[0, at, cols].astype(jnp.float32)
            outs[j][:, cols] = jnp.where(d * code > 0, d, 0.0).astype(jnp.bfloat16)


def base_input_body(place, bq, bkv, out, turned):
    transpose_columns(lambda c: keyval_tile(bkv, c), turned)
    rows = out.shape[0]
    at = pl.ds(pl.multiple_of(place[0] * rows, BLK), rows)
    out[:, :LANES] = bq[at, :]
    out[:, LANES:] = turned[at, :].astype(jnp.bfloat16)


def merged(base, parts):
    total = jnp.zeros(base.shape, jnp.float32)
    count = jnp.zeros(base.shape, jnp.float32)
    for part in parts:
        value = part.astype(jnp.float32)
        total = total + value
        count = count + jnp.where(value != 0, 1.0, 0.0)
    return (base.astype(jnp.float32) + total / jnp.maximum(count, 1.0)).astype(jnp.bfloat16)


def merge_input_body(base, *refs):
    out = refs[-1]
    step = BLK
    for r in range(out.shape[0] // step):
        at = slice(r * step, (r + 1) * step)
        out[at, :] = merged(base[at, :], [p[at, :] for p in refs[:-1]])


def merge_output_body(place, base, *refs):
    out = refs[-1]
    rows, width = out.shape
    at = pl.ds(pl.multiple_of(place[0] * rows, rows), rows)
    step = 4 * LANES
    for c in range(0, width, step):
        cols = slice(c, min(c + step, width))
        out[:, cols] = merged(base[at, cols], [p[:, cols] for p in refs[:-1]])


def turn(values, cosine, sine):
    return values * cosine + pltpu.roll(values, values.shape[-1] // 2, 1) * sine


def project_body(masks, tasks, place, normed, cosine, sine, *refs):
    pieces, q_out, kv_out = refs[:-2], refs[-2], refs[-1]
    total = jnp.zeros((q_out.shape[0], 2 * LANES), jnp.float32)
    for (tm, dm), piece in zip(masks, pieces):
        block = (place[1] ^ dm) * tasks + (place[0] ^ tm)
        total = total + jnp.dot(normed[block], piece[...], preferred_element_type=jnp.float32)
    q = turn(total[:, :LANES], cosine[...], sine[...])
    q_out[...] = (q * QUERY_SCALE).astype(jnp.bfloat16)
    kv_out[...] = total[:, LANES:].astype(jnp.bfloat16)


def join_body(place, cosine, sine, own, other, out):
    mine, theirs = own[...].astype(jnp.float32), other[...].astype(jnp.float32)
    even = place[2] % 2 == 0
    first = jnp.where(even, mine, theirs)
    second = jnp.where(even, theirs, mine)
    low = lax.broadcasted_iota(jnp.int32, first.shape, 1) < LANES // 2
    keys = jnp.where(low, first, pltpu.roll(second, LANES // 2, 1))
    values = jnp.where(low, pltpu.roll(first, LANES // 2, 1), second)
    out[:, :LANES] = turn(keys, cosine[...], sine[...]).astype(jnp.bfloat16)
    out[:, LANES:] = values.astype(jnp.bfloat16)


def attend_body(masks, halves, place, q_ref, *refs):
    pieces, out = refs[:-1], refs[-1]
    rows = q_ref.shape[0]
    q = q_ref[...]
    mine = place[0] * halves + place[1]
    row = lax.broadcasted_iota(jnp.int32, (rows, rows), 0)
    col = lax.broadcasted_iota(jnp.int32, (rows, rows), 1)
    top = jnp.zeros((rows, LANES), jnp.float32)
    bottom = jnp.zeros((rows, 1), jnp.float32)
    for (tm, dm), piece in zip(masks, pieces):
        theirs = (place[0] ^ tm) * halves + (place[1] ^ dm)
        scores = lax.dot_general(
            q, piece[:, :LANES], (((1,), (1,)), ((), ())), preferred_element_type=jnp.float32
        )
        capped = SCORE_CAP * jnp.tanh(scores / SCORE_CAP)
        allowed = col + theirs * rows <= row + mine * rows
        weights = jnp.where(allowed, jnp.exp(capped), 0.0)
        bottom = bottom + jnp.sum(weights, axis=1, keepdims=True)
        top = top + jnp.dot(
            weights.astype(jnp.bfloat16), piece[:, LANES:], preferred_element_type=jnp.float32
        )
    out[...] = (top / bottom).astype(jnp.bfloat16)


def output_body(masks, place, attention, *refs):
    pieces, out, whole = refs[:-2], refs[-2], refs[-1]
    for (tm, dm), piece in zip(masks, pieces):
        whole[place[1] ^ dm, place[0] ^ tm] = piece[...]
    halves, tasks, rows, width = whole.shape
    for h in range(halves):
        weight = whole[h].reshape(tasks * rows, width)
        out[:, h * width : (h + 1) * width] = jnp.dot(
            attention[...], weight, preferred_element_type=jnp.float32
        ).astype(jnp.bfloat16)


def rms_norm(values, gain):
    scale = lax.rsqrt(jnp.mean(values * values, axis=-1, keepdims=True) + EPSILON)
    return values * scale * gain


def on_device(
    hidden,
    pre_gain,
    base_query,
    base_keyval,
    base_output,
    delta_query,
    delta_keyval,
    delta_output,
    trim_query,
    trim_keyval,
    trim_output,
    sign_query,
    sign_keyval,
    sign_output,
    post_gain,
    final_gain,
    unembedding,
    targets,
    loss_mask,
):
    bf16, f32 = jnp.bfloat16, jnp.float32
    tasks = lax.axis_size("task")
    tensors = lax.axis_size("tensor")
    halves = lax.axis_size("dp")
    task, dp, tensor = lax.axis_index("task"), lax.axis_index("dp"), lax.axis_index("tensor")
    place = jnp.stack([task, dp, tensor]).astype(jnp.int32)
    row_count, width = hidden.shape
    half = base_query.shape[0]
    quarter = half // tasks
    out_rows = base_output.shape[0] // tasks

    kept_in = kernel_call(
        functools.partial(trim_input_body, tasks),
        [
            place,
            jnp.swapaxes(trim_query, 1, 2),
            jnp.swapaxes(trim_keyval, 2, 3),
            sign_query.T,
            jnp.swapaxes(sign_keyval, 1, 2),
            delta_query,
            jnp.swapaxes(delta_keyval, 2, 3),
        ],
        [SMEM] * 5 + [VMEM] * 2,
        [shape_of((quarter, 2 * LANES), bf16)] * tasks,
        [pltpu.VMEM((half, LANES), f32)],
        name="trim_input",
    )
    got_in = [kept_in[0]] + [swap(kept_in[j], "task", j) for j in range(1, tasks)]
    kept_out = kernel_call(
        functools.partial(trim_output_body, tasks),
        [place, trim_output, sign_output, delta_output],
        [SMEM] * 3 + [VMEM],
        [shape_of((out_rows, half), bf16)] * tasks,
        name="trim_output",
    )
    base_in = kernel_call(
        base_input_body,
        [place, base_query, jnp.swapaxes(base_keyval, 1, 2)],
        [SMEM] + [VMEM] * 2,
        [shape_of((quarter, 2 * LANES), bf16)],
        [pltpu.VMEM((half, LANES), f32)],
        name="base_input",
    )[0]

    residual = hidden.astype(f32)
    normed = rms_norm(residual, pre_gain).astype(bf16)
    blocks = width // quarter
    normed = jnp.transpose(normed.reshape(row_count, blocks, quarter), (1, 0, 2))
    group_index = task * halves + dp
    query_positions = group_index * row_count + jnp.arange(row_count, dtype=jnp.int32)
    half_head = LANES // 2
    frequencies = jnp.exp(
        -jnp.log(ROPE_BASE) * 2.0 * jnp.arange(half_head, dtype=jnp.int32).astype(f32) / LANES
    )
    angles = query_positions.astype(f32)[:, None] * frequencies[None, :]
    cosine, sine = jnp.cos(angles), jnp.sin(angles)
    cosine = jnp.concatenate([cosine, cosine], axis=1)
    sine = jnp.concatenate([-sine, sine], axis=1)

    piece_in = kernel_call(
        merge_input_body,
        [base_in] + got_in,
        [VMEM] * (1 + tasks),
        [shape_of((quarter, 2 * LANES), bf16)],
        name="merge_input",
    )[0]
    pieces_in = gather_group(piece_in)
    masks = [(tm, dm) for tm, dm, _ in pieces_in]

    ordered = lax.optimization_barrier(tuple(kept_out) + tuple(got_in))
    kept_out = ordered[:tasks]
    got_out = [kept_out[0]] + [swap(kept_out[j], "task", j) for j in range(1, tasks)]
    piece_out = kernel_call(
        merge_output_body,
        [place, base_output] + got_out,
        [SMEM] + [VMEM] * (1 + tasks),
        [shape_of((out_rows, half), bf16)],
        name="merge_output",
    )[0]

    queries, keyval = kernel_call(
        functools.partial(project_body, masks, tasks),
        [place, normed, cosine, sine] + [b for _, _, b in pieces_in],
        [SMEM] + [VMEM] * (3 + len(masks)),
        [shape_of((row_count, LANES), bf16)] * 2,
        flops=2 * row_count * width * 2 * LANES,
        name="project",
    )
    other = swap(keyval, "tensor", 1)
    joined = kernel_call(
        join_body,
        [place, cosine, sine, keyval, other],
        [SMEM] + [VMEM] * 4,
        [shape_of((row_count, 2 * LANES), bf16)],
        name="join",
    )[0]
    every_keyval = gather_group(joined)
    piece_out, _ = lax.optimization_barrier((piece_out, piece_in))
    pieces_out = gather_group(piece_out)
    attention = kernel_call(
        functools.partial(attend_body, masks, halves),
        [place, queries] + [b for _, _, b in every_keyval],
        [SMEM] + [VMEM] * (1 + len(masks)),
        [shape_of((row_count, LANES), bf16)],
        flops=4 * row_count * row_count * LANES * len(masks),
        transcendentals=2 * row_count * row_count * len(masks),
        name="attend",
    )[0]
    partial_value = kernel_call(
        functools.partial(output_body, masks),
        [place, attention] + [b for _, _, b in pieces_out],
        [SMEM] + [VMEM] * (1 + len(masks)),
        [shape_of((row_count, width), bf16)],
        [pltpu.VMEM((halves, tasks, out_rows, half), bf16)],
        flops=2 * row_count * width * LANES,
        name="output",
    )[0]

    span_rows = row_count // tensors
    share_rows = lax.psum_scatter(partial_value, "tensor", scatter_dimension=0, tiled=True).astype(f32)
    own_stream = lax.dynamic_slice_in_dim(residual, tensor * span_rows, span_rows, 0)
    stream = own_stream + rms_norm(share_rows, post_gain)
    final = rms_norm(stream, final_gain).astype(bf16)
    every_rows = lax.all_gather(final, ("task", "tensor", "dp"), axis=0, tiled=True)

    def order(values):
        return jnp.transpose(
            values.reshape(tasks, halves, tensors, span_rows), (0, 2, 1, 3)
        ).reshape(-1)

    ordered_targets, ordered_mask = order(targets), order(loss_mask)
    logits = lax.dot_general(
        every_rows, unembedding, (((1,), (1,)), ((), ())), preferred_element_type=f32
    )
    capped = LOGIT_CAP * jnp.tanh(logits / LOGIT_CAP)
    vocab_ids = lax.axis_index(("task", "tensor", "dp")) * unembedding.shape[0] + jnp.arange(
        unembedding.shape[0], dtype=jnp.int32
    )
    local_sumexp = jnp.sum(jnp.exp(capped), axis=1)
    local_target = jnp.sum(
        jnp.where(ordered_targets[:, None] == vocab_ids[None, :], capped, 0.0), axis=1
    )
    both = jnp.stack([local_sumexp, local_target])
    both = total_over_group(total_over(both, "tensor"))
    sumexp, target_logit = both[0], both[1]
    counted = ordered_mask.astype(f32)
    losses = (jnp.log(sumexp) - target_logit) * counted
    summary = jnp.stack([jnp.sum(losses), jnp.sum(counted)])
    losses = jnp.transpose(
        losses.reshape(tasks, tensors, halves, span_rows), (0, 2, 1, 3)
    ).reshape(-1)
    own_losses = lax.dynamic_slice_in_dim(losses, group_index * row_count, row_count, 0)
    return (own_losses, summary)


def solution(mesh):
    return jax.shard_map(
        on_device,
        mesh=mesh,
        in_specs=(
            P(("task", "dp"), None),
            P(),
            P("dp", "tensor"),
            P(None, "dp", "tensor"),
            P("tensor", "dp"),
            P("task", "dp", "tensor"),
            P("task", None, "dp", "tensor"),
            P("task", "tensor", "dp"),
            P("task", "dp", "tensor"),
            P("task", None, "dp", "tensor"),
            P("task", "tensor", "dp"),
            P("dp", "tensor"),
            P(None, "dp", "tensor"),
            P("tensor", "dp"),
            P(),
            P(),
            P(("task", "tensor", "dp"), None),
            P(),
            P(),
        ),
        out_specs=(P(("task", "dp")), P()),
        check_vma=False,
    )
```

```python
import functools

import jax
import jax.numpy as jnp
from jax import lax
from jax.experimental import pallas as pl
from jax.experimental.pallas import tpu as pltpu
from jax.sharding import PartitionSpec as P


BLK = 64
LANES = 128

EPSILON = 1e-06
QUERY_SCALE = 1.0 / 12.0
ROPE_BASE = 10000.0
SCORE_CAP = 50.0
LOGIT_CAP = 30.0


VMEM = pl.BlockSpec(memory_space=pltpu.VMEM)
SMEM = pl.BlockSpec(memory_space=pltpu.SMEM)


def kernel_call(body, inputs, in_specs, outputs, scratch=(), flops=1, transcendentals=0):
    moved = sum(a.size * a.dtype.itemsize for a in inputs)
    moved += sum(int(jnp.dtype(o.dtype).itemsize) * o.size for o in outputs)
    return pl.pallas_call(
        body,
        out_shape=outputs,
        in_specs=in_specs,
        out_specs=[VMEM] * len(outputs),
        scratch_shapes=list(scratch),
        cost_estimate=pl.CostEstimate(
            flops=flops, bytes_accessed=moved, transcendentals=transcendentals
        ),
    )(*inputs)


def shape_of(dims, dtype):
    return jax.ShapeDtypeStruct(tuple(dims), dtype)


def swap(block, axis, mask):
    count = lax.axis_size(axis)
    return lax.ppermute(block, axis, [(i, i ^ mask) for i in range(count)])


def swap_two(block, task_mask, dp_mask):
    tasks, halves = lax.axis_size("task"), lax.axis_size("dp")
    route = []
    for t in range(tasks):
        for d in range(halves):
            route.append((t * halves + d, (t ^ task_mask) * halves + (d ^ dp_mask)))
    return lax.ppermute(block, ("task", "dp"), route)


def gather_group(block):
    tasks, halves = lax.axis_size("task"), lax.axis_size("dp")
    near = [(0, 0, block)]
    for tm in range(0, tasks, 2):
        for dm in range(halves):
            if tm or dm:
                if not dm:
                    got = swap(block, "task", tm)
                elif not tm:
                    got = swap(block, "dp", dm)
                else:
                    got = swap_two(block, tm, dm)
                near.append((tm, dm, got))
    return near + [(tm ^ 1, dm, swap(b, "task", 1)) for tm, dm, b in near]


def after(values, earlier):
    count = len(values)
    return list(lax.optimization_barrier(tuple(values) + tuple(earlier))[:count])


def total_over(value, axis):
    count = lax.axis_size(axis)
    if count <= 4:
        parts = [swap(value, axis, m) for m in range(1, count)]
        for part in parts:
            value = value + part
        return value
    step = 1
    while step < count:
        value = value + swap(value, axis, step)
        step *= 2
    return value


def total_over_group(value):
    tasks, halves = lax.axis_size("task"), lax.axis_size("dp")
    parts = []
    for tm in range(0, tasks, 2):
        for dm in range(halves):
            if tm or dm:
                parts.append(swap_two(value, tm, dm))
    for part in parts:
        value = value + part
    return value + swap(value, "task", 1)


def block_code(trim, sign):
    return (trim * (2 * sign - 1)).astype(jnp.float32)


def transpose_columns(source, out_ref):
    for c in range(out_ref.shape[0] // LANES):
        out_ref[c * LANES : (c + 1) * LANES, :] = source(c).astype(jnp.float32).T


def keyval_tile(ref, c):
    both = ref[:, :, c * LANES : (c + 1) * LANES]
    return both.reshape(2 * both.shape[1], LANES)


def trim_input_body(tasks, place, tq, tkv, sq, skv, dq, dkv, *rest):
    outs, turned = rest[:-1], rest[-1]
    me = place[0]
    transpose_columns(lambda c: keyval_tile(dkv.at[0], c), turned)
    rows = outs[0].shape[0]
    blocks = rows // BLK
    low = lax.broadcasted_iota(jnp.int32, (BLK, LANES), 1) < BLK
    for j in range(tasks):
        first = (me ^ j) * blocks
        for r in range(blocks):
            b = first + r
            at = pl.ds(pl.multiple_of(b * BLK, BLK), BLK)
            here = slice(r * BLK, (r + 1) * BLK)
            code = jnp.where(
                low, block_code(tq[0, 0, b], sq[0, b]), block_code(tq[0, 1, b], sq[1, b])
            )
            d = dq[0, at, :].astype(jnp.float32)
            outs[j][here, :LANES] = jnp.where(d * code > 0, d, 0.0).astype(jnp.bfloat16)
            code = jnp.where(
                low, block_code(tkv[0, 0, 0, b], skv[0, 0, b]), block_code(tkv[0, 1, 0, b], skv[1, 0, b])
            )
            d = turned[at, :]
            outs[j][here, LANES:] = jnp.where(d * code > 0, d, 0.0).astype(jnp.bfloat16)


def trim_output_body(tasks, place, to, so, do, *outs):
    me = place[0]
    rows, width = outs[0].shape
    low = lax.broadcasted_iota(jnp.int32, (rows, LANES), 1) < BLK
    for j in range(tasks):
        first = (me ^ j) * rows
        at = pl.ds(pl.multiple_of(first, rows), rows)
        b = first // BLK
        for c in range(width // LANES):
            cols = slice(c * LANES, (c + 1) * LANES)
            code = jnp.where(
                low,
                block_code(to[0, b, 2 * c], so[b, 2 * c]),
                block_code(to[0, b, 2 * c + 1], so[b, 2 * c + 1]),
            )
            d = do[0, at, cols].astype(jnp.float32)
            outs[j][:, cols] = jnp.where(d * code > 0, d, 0.0).astype(jnp.bfloat16)


def base_input_body(place, bq, bkv, out, turned):
    transpose_columns(lambda c: keyval_tile(bkv, c), turned)
    rows = out.shape[0]
    at = pl.ds(pl.multiple_of(place[0] * rows, BLK), rows)
    out[:, :LANES] = bq[at, :]
    out[:, LANES:] = turned[at, :].astype(jnp.bfloat16)


def merged(base, parts, gain=1.0):
    total = jnp.zeros(base.shape, jnp.float32)
    count = jnp.zeros(base.shape, jnp.float32)
    for part in parts:
        value = part.astype(jnp.float32)
        total = total + value
        count = count + jnp.where(value != 0, 1.0, 0.0)
    value = base.astype(jnp.float32) + total / jnp.maximum(count, 1.0)
    return (value * gain).astype(jnp.bfloat16)


def merge_input_body(base, *refs):
    out = refs[-1]
    step = BLK
    for r in range(out.shape[0] // step):
        at = slice(r * step, (r + 1) * step)
        out[at, :] = merged(base[at, :], [p[at, :] for p in refs[:-1]])


def merge_output_body(place, gain, base, *refs):
    out = refs[-1]
    rows, width = out.shape
    start = place[1] * width
    at = pl.ds(pl.multiple_of(place[0] * rows, rows), rows)
    step = 4 * LANES
    for c in range(0, width, step):
        cols = slice(c, min(c + step, width))
        size = min(c + step, width) - c
        factor = gain[0:1, pl.ds(pl.multiple_of(start + c, LANES), size)]
        out[:, cols] = merged(base[at, cols], [p[:, cols] for p in refs[:-1]], factor)


def turn(values, cosine, sine):
    return values * cosine + pltpu.roll(values, values.shape[-1] // 2, 1) * sine


def project_body(masks, tasks, place, normed, cosine, sine, *refs):
    pieces, q_out, kv_out = refs[:-2], refs[-2], refs[-1]
    total = jnp.zeros((q_out.shape[0], 2 * LANES), jnp.float32)
    for (tm, dm), piece in zip(masks, pieces):
        block = (place[1] ^ dm) * tasks + (place[0] ^ tm)
        total = total + jnp.dot(normed[block], piece[...], preferred_element_type=jnp.float32)
    q = turn(total[:, :LANES], cosine[...], sine[...])
    q_out[...] = (q * QUERY_SCALE).astype(jnp.bfloat16)
    kv_out[...] = total[:, LANES:].astype(jnp.bfloat16)


def join_body(place, cosine, sine, own, other, out):
    mine, theirs = own[...].astype(jnp.float32), other[...].astype(jnp.float32)
    even = place[2] % 2 == 0
    first = jnp.where(even, mine, theirs)
    second = jnp.where(even, theirs, mine)
    low = lax.broadcasted_iota(jnp.int32, first.shape, 1) < LANES // 2
    keys = jnp.where(low, first, pltpu.roll(second, LANES // 2, 1))
    values = jnp.where(low, pltpu.roll(first, LANES // 2, 1), second)
    out[:, :LANES] = turn(keys, cosine[...], sine[...]).astype(jnp.bfloat16)
    out[:, LANES:] = values.astype(jnp.bfloat16)


def attend_body(masks, halves, place, q_ref, *refs):
    pieces, out = refs[:-1], refs[-1]
    rows = q_ref.shape[0]
    q = q_ref[...]
    mine = place[0] * halves + place[1]
    row = lax.broadcasted_iota(jnp.int32, (rows, rows), 0)
    col = lax.broadcasted_iota(jnp.int32, (rows, rows), 1)
    top = jnp.zeros((rows, LANES), jnp.float32)
    bottom = jnp.zeros((rows, 1), jnp.float32)
    for (tm, dm), piece in zip(masks, pieces):
        theirs = (place[0] ^ tm) * halves + (place[1] ^ dm)
        scores = lax.dot_general(
            q, piece[:, :LANES], (((1,), (1,)), ((), ())), preferred_element_type=jnp.float32
        )
        capped = SCORE_CAP * jnp.tanh(scores / SCORE_CAP)
        allowed = col + theirs * rows <= row + mine * rows
        weights = jnp.where(allowed, jnp.exp(capped), 0.0)
        bottom = bottom + jnp.sum(weights, axis=1, keepdims=True)
        top = top + jnp.dot(
            weights.astype(jnp.bfloat16), piece[:, LANES:], preferred_element_type=jnp.float32
        )
    out[...] = (top / bottom).astype(jnp.bfloat16)


def output_body(masks, place, attention, *refs):
    pieces, out, whole = refs[:-2], refs[-2], refs[-1]
    for (tm, dm), piece in zip(masks, pieces):
        whole[place[1] ^ dm, place[0] ^ tm] = piece[...]
    halves, tasks, rows, width = whole.shape
    for h in range(halves):
        weight = whole[h].reshape(tasks * rows, width)
        out[:, h * width : (h + 1) * width] = jnp.dot(
            attention[...], weight, preferred_element_type=jnp.float32
        ).astype(jnp.bfloat16)


def heads_body(masks, place, *refs):
    parts, out = refs[:-1], refs[-1]
    for m, part in zip(masks, parts):
        out[:, pl.ds(pl.multiple_of((place[2] ^ m) * LANES, LANES), LANES)] = part[...]


def assemble_body(labels, place, *refs):
    pieces, plain = refs[:-1], refs[-1]
    rows, half = plain.shape[2], pieces[0].shape[1]
    for (tm, dm, first), piece in zip(labels, pieces):
        h, t = place[1] ^ dm, place[0] ^ tm
        cols = pl.ds(pl.multiple_of(h * half, LANES), half)
        for m in range(piece.shape[0] // rows):
            plain[place[2] ^ (first + m), t, :, cols] = piece[m * rows : (m + 1) * rows, :]


def statistics_body(attention, weight, hidden, to_plain, to_post, out):
    rows, width = hidden.shape
    step = width // 4
    squares = jnp.zeros((rows, 1), jnp.float32)
    parts = []
    for c in range(0, width, step):
        p = jnp.dot(
            attention[...], weight[:, c : c + step], preferred_element_type=jnp.float32
        )
        plain = p * to_plain[0:1, c : c + step]
        squares = squares + jnp.sum(plain * plain, axis=1, keepdims=True)
        parts.append(p)
    inner = lax.rsqrt(squares / width + EPSILON)
    squares = jnp.zeros((rows, 1), jnp.float32)
    for i, p in enumerate(parts):
        cols = slice(i * step, (i + 1) * step)
        stream = hidden[:, cols].astype(jnp.float32) + p * inner * to_post[0:1, cols]
        squares = squares + jnp.sum(stream * stream, axis=1, keepdims=True)
    outer = lax.rsqrt(squares / width + EPSILON)
    lane = lax.broadcasted_iota(jnp.int32, (rows, LANES), 1)
    table = jnp.where(lane == 0, inner, jnp.where(lane == 1, outer, 0.0))
    out[...] = table.T[: out.shape[0], :]


def contract_body(count, table, *refs):
    left, out, total = refs[:count], refs[count], refs[count + 1]
    step = pl.program_id(0)
    rows = [ref[...] for ref in left]
    product = lax.dot_general(
        jnp.concatenate(rows, axis=0) if count > 1 else rows[0],
        table[...],
        (((1,), (1,)), ((), ())),
        preferred_element_type=jnp.float32,
    )

    @pl.when(step == 0)
    def _():
        total[...] = product

    @pl.when(step > 0)
    def _():
        total[...] += product

    @pl.when(step == pl.num_programs(0) - 1)
    def _():
        out[...] = total[...].astype(out.dtype)


def contract(left, table, dtype):
    width = table.shape[1]
    step = width // 4 if width % (4 * LANES) == 0 else width
    rows = sum(block.shape[0] for block in left)
    vocab = table.shape[0]
    return pl.pallas_call(
        functools.partial(contract_body, len(left)),
        out_shape=shape_of((rows, vocab), dtype),
        grid=(width // step,),
        in_specs=[pl.BlockSpec((vocab, step), lambda k: (0, k))]
        + [pl.BlockSpec((block.shape[0], step), lambda k: (0, k)) for block in left],
        out_specs=pl.BlockSpec((rows, vocab), lambda k: (0, 0)),
        scratch_shapes=[pltpu.VMEM((rows, vocab), jnp.float32)],
        name="contract",
        cost_estimate=pl.CostEstimate(
            flops=2 * rows * width * vocab,
            bytes_accessed=2 * (rows + vocab) * width + 4 * rows * vocab,
            transcendentals=0,
        ),
    )(table, *left)


def score_body(masks, halves, place, targets, mixed, *refs):
    count = len(masks)
    attention, stats = refs[:count], refs[count : 2 * count]
    near, far, out = refs[2 * count :]
    rows = attention[0].shape[0]
    vocab = mixed.shape[1]
    first_id = place[3]
    lane = lax.broadcasted_iota(jnp.int32, (rows, LANES), 1)
    for n, (tm, dm) in enumerate(masks):
        group = (place[0] ^ tm) * halves + (place[1] ^ dm)
        table = stats[n][...].T
        wanted = jnp.broadcast_to(targets[pl.ds(group, 1), :], (8, rows)).T
        inner, outer, wanted = table[:, 0:1], table[:, 1:2], wanted[:, 0:1]
        base = far if tm > 1 else near
        start = (halves * (tm % 2) + dm) * rows
        sums = jnp.zeros((rows, LANES), jnp.float32)
        hits = jnp.zeros((rows, LANES), jnp.float32)
        product = jnp.dot(attention[n][...], mixed[...], preferred_element_type=jnp.float32)
        for v in range(vocab // LANES):
            cols = slice(v * LANES, (v + 1) * LANES)
            logits = outer * (base[start : start + rows, cols] + inner * product[:, cols])
            capped = LOGIT_CAP * jnp.tanh(logits / LOGIT_CAP)
            sums = sums + jnp.exp(capped)
            hits = hits + jnp.where(lane + (first_id + v * LANES) == wanted, capped, 0.0)
        for kind, value in ((0, sums), (1, hits)):
            out[kind, pl.ds(group, 1), :] = jnp.sum(value.T, axis=0, keepdims=True)


def loss_body(halves, place, mask, first, second, own, summary):
    both = first[...] + second[...]
    counted = mask[...].astype(jnp.float32)
    losses = (jnp.log(both[0]) - both[1]) * counted
    at = pl.ds(place[0] * halves + place[1], 1)
    sumexp = first[0, at, :] + second[0, at, :]
    target = first[1, at, :] + second[1, at, :]
    own[...] = (jnp.log(sumexp) - target) * mask[at, :].astype(jnp.float32)
    summary[0] = jnp.sum(losses)
    summary[1] = jnp.sum(counted)


def rms_norm(values, gain):
    scale = lax.rsqrt(jnp.mean(values * values, axis=-1, keepdims=True) + EPSILON)
    return values * scale * gain


def general_tail(
    place, masks, attention, piece_out, hidden, post_gain, final_gain, unembedding, targets, loss_mask
):
    bf16, f32 = jnp.bfloat16, jnp.float32
    tasks = lax.axis_size("task")
    tensors = lax.axis_size("tensor")
    halves = lax.axis_size("dp")
    task, dp, tensor = lax.axis_index("task"), lax.axis_index("dp"), lax.axis_index("tensor")
    row_count, width = hidden.shape
    out_rows, half = piece_out.shape
    residual = hidden.astype(f32)
    group_index = task * halves + dp
    pieces_out = gather_group(piece_out)
    partial_value = kernel_call(
        functools.partial(output_body, masks),
        [place, attention] + [b for _, _, b in pieces_out],
        [SMEM] + [VMEM] * (1 + len(masks)),
        [shape_of((row_count, width), bf16)],
        [pltpu.VMEM((halves, tasks, out_rows, half), bf16)],
        flops=2 * row_count * width * LANES,
    )[0]

    span_rows = row_count // tensors
    share_rows = lax.psum_scatter(partial_value, "tensor", scatter_dimension=0, tiled=True).astype(f32)
    own_stream = lax.dynamic_slice_in_dim(residual, tensor * span_rows, span_rows, 0)
    stream = own_stream + rms_norm(share_rows, post_gain)
    final = rms_norm(stream, final_gain).astype(bf16)
    every_rows = lax.all_gather(final, ("task", "tensor", "dp"), axis=0, tiled=True)

    def order(values):
        return jnp.transpose(
            values.reshape(tasks, halves, tensors, span_rows), (0, 2, 1, 3)
        ).reshape(-1)

    ordered_targets, ordered_mask = order(targets), order(loss_mask)
    logits = lax.dot_general(
        every_rows, unembedding, (((1,), (1,)), ((), ())), preferred_element_type=f32
    )
    capped = LOGIT_CAP * jnp.tanh(logits / LOGIT_CAP)
    vocab_ids = lax.axis_index(("task", "tensor", "dp")) * unembedding.shape[0] + jnp.arange(
        unembedding.shape[0], dtype=jnp.int32
    )
    local_sumexp = jnp.sum(jnp.exp(capped), axis=1)
    local_target = jnp.sum(
        jnp.where(ordered_targets[:, None] == vocab_ids[None, :], capped, 0.0), axis=1
    )
    both = jnp.stack([local_sumexp, local_target])
    both = total_over_group(total_over(both, "tensor"))
    sumexp, target_logit = both[0], both[1]
    counted = ordered_mask.astype(f32)
    losses = (jnp.log(sumexp) - target_logit) * counted
    summary = jnp.stack([jnp.sum(losses), jnp.sum(counted)])
    losses = jnp.transpose(
        losses.reshape(tasks, tensors, halves, span_rows), (0, 2, 1, 3)
    ).reshape(-1)
    own_losses = lax.dynamic_slice_in_dim(losses, group_index * row_count, row_count, 0)
    return (own_losses, summary)


def exchange_hidden(hidden, kept, tensor):
    tensors = lax.axis_size("tensor")
    rows = hidden.shape[0] // tensors
    cut = hidden.shape[0] // 2
    hidden = after([hidden], [kept])[0]
    share = lax.dynamic_slice_in_dim(hidden, tensor * rows, rows, 0)
    top, bottom = hidden[:cut], hidden[cut:]
    dp_top = swap(top, "dp", 1)
    by_task = swap(share, "task", 2)
    dp_bottom = swap(bottom, "dp", 1)
    task_all = jnp.zeros_like(hidden)
    for m in range(tensors):
        block = swap(by_task, "tensor", m) if m else by_task
        task_all = lax.dynamic_update_slice_in_dim(task_all, block, (tensor ^ m) * rows, 0)
    both_top = swap(dp_top, "task", 2)
    both_bottom = swap(task_all[cut:], "dp", 1)

    def paired(blocks):
        return blocks + [swap(block, "task", 1) for block in blocks]

    return paired([hidden, dp_top, dp_bottom]), paired([task_all, both_top, both_bottom])


def split_tail(
    where,
    attention,
    piece_out,
    inverse_gains,
    far_rows,
    near,
    hidden,
    unembedding,
    targets,
    loss_mask,
):
    bf16, f32 = jnp.bfloat16, jnp.float32
    tasks = lax.axis_size("task")
    tensors = lax.axis_size("tensor")
    halves = lax.axis_size("dp")
    row_count, width = hidden.shape
    out_rows, _ = piece_out.shape
    groups = tasks * halves
    vocab = unembedding.shape[0]
    place = where
    to_plain, to_post = inverse_gains

    column = jnp.concatenate([piece_out] + [swap(piece_out, "tensor", m) for m in range(1, tensors)], axis=0)
    by_task, by_dp = swap(column, "task", 2), swap(column, "dp", 1)
    cut = column.shape[0] // 2
    parts = [
        (0, 0, 0, column),
        (2, 0, 0, by_task),
        (0, 1, 0, by_dp),
        (2, 1, 0, swap(by_dp[:cut], "task", 2)),
        (2, 1, cut // out_rows, swap(by_task[cut:], "dp", 1)),
    ]
    parts += [(tm ^ 1, dm, first, swap(b, "task", 1)) for tm, dm, first, b in parts]
    plain = kernel_call(
        functools.partial(assemble_body, [part[:3] for part in parts]),
        [place] + [part[3] for part in parts],
        [SMEM] + [VMEM] * len(parts),
        [shape_of((tensors, tasks, out_rows, width), bf16)],
    )[0]
    features = tensors * tasks * out_rows
    plain = plain.reshape(features, width)
    mixed = contract([plain], unembedding, bf16)

    heads = kernel_call(
        functools.partial(heads_body, list(range(tensors))),
        [place, attention] + [swap(attention, "tensor", m) for m in range(1, tensors)],
        [SMEM] + [VMEM] * tensors,
        [shape_of((row_count, features), bf16)],
    )[0]
    stats = kernel_call(
        statistics_body,
        [heads, plain, hidden, to_plain, to_post],
        [VMEM] * 5,
        [shape_of((8, row_count), f32)],
        flops=2 * row_count * features * width,
    )[0]
    every_heads = gather_group(heads)
    far = contract(far_rows, unembedding, f32)
    every_stats = gather_group(stats)
    both = kernel_call(
        functools.partial(score_body, [(tm, dm) for tm, dm, _ in every_heads], halves),
        [where, targets.reshape(groups, row_count), mixed]
        + [b for _, _, b in every_heads]
        + [b for _, _, b in every_stats]
        + [near, far],
        [SMEM] + [VMEM] * (4 + 2 * groups),
        [shape_of((2, groups, row_count), f32)],
        flops=2 * groups * row_count * features * vocab,
        transcendentals=2 * groups * row_count * vocab,
    )[0]
    both = total_over(both, "tensor")
    parts = [swap_two(both, tm, dm) for tm in range(0, tasks, 2) for dm in range(halves) if tm or dm]
    for part in parts:
        both = both + part
    own, summary = pl.pallas_call(
        functools.partial(loss_body, halves),
        out_shape=[shape_of((1, row_count), f32), shape_of((2,), f32)],
        in_specs=[SMEM] + [VMEM] * 3,
        out_specs=[VMEM, SMEM],
        name="loss",
    )(place, loss_mask.reshape(groups, row_count), both, swap(both, "task", 1))
    return own.reshape(row_count), summary


def on_device(
    hidden,
    pre_gain,
    base_query,
    base_keyval,
    base_output,
    delta_query,
    delta_keyval,
    delta_output,
    trim_query,
    trim_keyval,
    trim_output,
    sign_query,
    sign_keyval,
    sign_output,
    post_gain,
    final_gain,
    unembedding,
    targets,
    loss_mask,
):
    bf16, f32 = jnp.bfloat16, jnp.float32
    tasks = lax.axis_size("task")
    tensors = lax.axis_size("tensor")
    halves = lax.axis_size("dp")
    task, dp, tensor = lax.axis_index("task"), lax.axis_index("dp"), lax.axis_index("tensor")
    place = jnp.stack([task, dp, tensor]).astype(jnp.int32)
    row_count, width = hidden.shape
    half = base_query.shape[0]
    quarter = half // tasks
    out_rows = base_output.shape[0] // tasks

    kept_in = kernel_call(
        functools.partial(trim_input_body, tasks),
        [
            place,
            jnp.swapaxes(trim_query, 1, 2),
            jnp.swapaxes(trim_keyval, 2, 3),
            sign_query.T,
            jnp.swapaxes(sign_keyval, 1, 2),
            delta_query,
            jnp.swapaxes(delta_keyval, 2, 3),
        ],
        [SMEM] * 5 + [VMEM] * 2,
        [shape_of((quarter, 2 * LANES), bf16)] * tasks,
        [pltpu.VMEM((half, LANES), f32)],
    )
    got_in = [kept_in[0]] + [swap(kept_in[j], "task", j) for j in range(1, tasks)]
    kept_out = kernel_call(
        functools.partial(trim_output_body, tasks),
        [place, trim_output, sign_output, delta_output],
        [SMEM] * 3 + [VMEM],
        [shape_of((out_rows, half), bf16)] * tasks,
    )
    base_in = kernel_call(
        base_input_body,
        [place, base_query, jnp.swapaxes(base_keyval, 1, 2)],
        [SMEM] + [VMEM] * 2,
        [shape_of((quarter, 2 * LANES), bf16)],
        [pltpu.VMEM((half, LANES), f32)],
    )[0]

    residual = hidden.astype(f32)
    normed = rms_norm(residual, pre_gain).astype(bf16)
    blocks = width // quarter
    normed = jnp.transpose(normed.reshape(row_count, blocks, quarter), (1, 0, 2))
    group_index = task * halves + dp
    query_positions = group_index * row_count + jnp.arange(row_count, dtype=jnp.int32)
    half_head = LANES // 2
    frequencies = jnp.exp(
        -jnp.log(ROPE_BASE) * 2.0 * jnp.arange(half_head, dtype=jnp.int32).astype(f32) / LANES
    )
    angles = query_positions.astype(f32)[:, None] * frequencies[None, :]
    cosine, sine = jnp.cos(angles), jnp.sin(angles)
    cosine = jnp.concatenate([cosine, cosine], axis=1)
    sine = jnp.concatenate([-sine, sine], axis=1)

    gathered_bytes = tensors * base_output.shape[0] * width * base_output.dtype.itemsize
    low_rank = gathered_bytes <= 6 * 2**20
    where = jnp.concatenate(
        [place, (lax.axis_index(("task", "tensor", "dp")) * unembedding.shape[0]).astype(jnp.int32)[None]]
    )
    if low_rank:
        weight_gain = (post_gain * final_gain)[None, :]
        rows = [weight_gain, 1.0 / weight_gain, (1.0 / final_gain)[None, :], where]
    else:
        rows = [jnp.ones((1, width), f32), where]
    tied = after(list(got_in) + rows, [])
    got_in, rows = tied[:tasks], tied[tasks:]
    weight_gain, where = rows[0], rows[-1]
    piece_in = kernel_call(
        merge_input_body,
        [base_in] + got_in,
        [VMEM] * (1 + tasks),
        [shape_of((quarter, 2 * LANES), bf16)],
    )[0]
    pieces_in = gather_group(piece_in)
    masks = [(tm, dm) for tm, dm, _ in pieces_in]

    kept_out = after(kept_out, [piece_in])
    got_out = [kept_out[0]] + [swap(kept_out[j], "task", j) for j in range(1, tasks)]
    got_out = after(got_out, [b for _, _, b in pieces_in[1:4]])
    if low_rank:
        scaled = (hidden.astype(f32) * final_gain).astype(bf16)
        near_rows, far_rows = exchange_hidden(scaled, kept_in[0], tensor)
        near_rows = after(near_rows, [piece_in])
        near = contract(near_rows, unembedding, f32)
    piece_out = kernel_call(
        merge_output_body,
        [place, weight_gain, base_output] + got_out,
        [SMEM] + [VMEM] * (2 + tasks),
        [shape_of((out_rows, half), bf16)],
    )[0]

    queries, keyval = kernel_call(
        functools.partial(project_body, masks, tasks),
        [place, normed, cosine, sine] + [b for _, _, b in pieces_in],
        [SMEM] + [VMEM] * (3 + len(masks)),
        [shape_of((row_count, LANES), bf16)] * 2,
        flops=2 * row_count * width * 2 * LANES,
    )
    other = swap(keyval, "tensor", 1)
    joined = kernel_call(
        join_body,
        [place, cosine, sine, keyval, other],
        [SMEM] + [VMEM] * 4,
        [shape_of((row_count, 2 * LANES), bf16)],
    )[0]
    every_keyval = gather_group(joined)
    if low_rank:
        queries = after([queries], [near])[0]
    attention = kernel_call(
        functools.partial(attend_body, masks, halves),
        [place, queries] + [b for _, _, b in every_keyval],
        [SMEM] + [VMEM] * (1 + len(masks)),
        [shape_of((row_count, LANES), bf16)],
        flops=4 * row_count * row_count * LANES * len(masks),
        transcendentals=2 * row_count * row_count * len(masks),
    )[0]
    if not low_rank:
        return general_tail(
            place, masks, attention, piece_out, hidden, post_gain, final_gain, unembedding, targets, loss_mask
        )
    return split_tail(
        where,
        attention,
        piece_out,
        rows[1:3],
        far_rows,
        near,
        hidden,
        unembedding,
        targets,
        loss_mask,
    )


def solution(mesh):
    return jax.shard_map(
        on_device,
        mesh=mesh,
        in_specs=(
            P(("task", "dp"), None),
            P(),
            P("dp", "tensor"),
            P(None, "dp", "tensor"),
            P("tensor", "dp"),
            P("task", "dp", "tensor"),
            P("task", None, "dp", "tensor"),
            P("task", "tensor", "dp"),
            P("task", "dp", "tensor"),
            P("task", None, "dp", "tensor"),
            P("task", "tensor", "dp"),
            P("dp", "tensor"),
            P(None, "dp", "tensor"),
            P("tensor", "dp"),
            P(),
            P(),
            P(("task", "tensor", "dp"), None),
            P(),
            P(),
        ),
        out_specs=(P(("task", "dp")), P()),
        check_vma=False,
    )
```

```python
import functools

import jax
import jax.numpy as jnp
from jax import lax
from jax.experimental import pallas as pl
from jax.experimental.pallas import tpu as pltpu
from jax.sharding import PartitionSpec as P


TASK, TENSOR, DP = "task", "tensor", "dp"

BLK = 64
LANES = 128

EPSILON = 1e-06
QUERY_SCALE = 1.0 / 12.0
ROPE_BASE = 10000.0
SCORE_CAP = 50.0
LOGIT_CAP = 30.0


KERNEL_VMEM = 20 * 2**20
CONTRACT_VMEM = 28 * 2**20

VMEM = pl.BlockSpec(memory_space=pltpu.VMEM)
SMEM = pl.BlockSpec(memory_space=pltpu.SMEM)


def kernel_call(body, inputs, in_specs, outputs, scratch=(), flops=1, transcendentals=0):
    moved = sum(a.size * a.dtype.itemsize for a in inputs)
    moved += sum(int(jnp.dtype(o.dtype).itemsize) * o.size for o in outputs)
    return pl.pallas_call(
        body,
        out_shape=outputs,
        in_specs=in_specs,
        out_specs=[VMEM] * len(outputs),
        scratch_shapes=list(scratch),
        compiler_params=pltpu.CompilerParams(vmem_limit_bytes=KERNEL_VMEM),
        cost_estimate=pl.CostEstimate(
            flops=flops, bytes_accessed=moved, transcendentals=transcendentals
        ),
    )(*inputs)


def shape_of(dims, dtype):
    return jax.ShapeDtypeStruct(tuple(dims), dtype)


def swap(block, axis, mask):
    count = lax.axis_size(axis)
    return lax.ppermute(block, axis, [(i, i ^ mask) for i in range(count)])


def swap_two(block, task_mask, dp_mask):
    tasks, halves = lax.axis_size(TASK), lax.axis_size(DP)
    route = []
    for t in range(tasks):
        for d in range(halves):
            route.append((t * halves + d, (t ^ task_mask) * halves + (d ^ dp_mask)))
    return lax.ppermute(block, (TASK, DP), route)


def gather_group(block):
    tasks, halves = lax.axis_size(TASK), lax.axis_size(DP)
    near = [(0, 0, block)]
    for tm in range(0, tasks, 2):
        for dm in range(halves):
            if tm or dm:
                if not dm:
                    got = swap(block, TASK, tm)
                elif not tm:
                    got = swap(block, DP, dm)
                else:
                    got = swap_two(block, tm, dm)
                near.append((tm, dm, got))
    return near + [(tm ^ 1, dm, swap(b, TASK, 1)) for tm, dm, b in near]


def after(values, earlier):
    count = len(values)
    return list(lax.optimization_barrier(tuple(values) + tuple(earlier))[:count])


def total_over(value, axis):
    count = lax.axis_size(axis)
    if count <= 4:
        parts = [swap(value, axis, m) for m in range(1, count)]
        for part in parts:
            value = value + part
        return value
    step = 1
    while step < count:
        value = value + swap(value, axis, step)
        step *= 2
    return value


def total_over_group(value):
    tasks, halves = lax.axis_size(TASK), lax.axis_size(DP)
    parts = []
    for tm in range(0, tasks, 2):
        for dm in range(halves):
            if tm or dm:
                parts.append(swap_two(value, tm, dm))
    for part in parts:
        value = value + part
    return value + swap(value, TASK, 1)


def block_code(trim, sign):
    return (trim * (2 * sign - 1)).astype(jnp.float32)


def transpose_columns(source, out_ref):
    for c in range(out_ref.shape[0] // LANES):
        out_ref[c * LANES : (c + 1) * LANES, :] = source(c).astype(jnp.float32).T


def keyval_tile(ref, c):
    both = ref[:, :, c * LANES : (c + 1) * LANES]
    return both.reshape(2 * both.shape[1], LANES)


def trim_input_body(tasks, place, tq, tkv, sq, skv, dq, dkv, *rest):
    outs, turned = rest[:-1], rest[-1]
    me = place[0]
    transpose_columns(lambda c: keyval_tile(dkv.at[0], c), turned)
    rows = outs[0].shape[0]
    blocks = rows // BLK
    low = lax.broadcasted_iota(jnp.int32, (BLK, LANES), 1) < BLK
    for j in range(tasks):
        first = (me ^ j) * blocks
        for r in range(blocks):
            b = first + r
            at = pl.ds(pl.multiple_of(b * BLK, BLK), BLK)
            here = slice(r * BLK, (r + 1) * BLK)
            code = jnp.where(
                low, block_code(tq[0, 0, b], sq[0, b]), block_code(tq[0, 1, b], sq[1, b])
            )
            d = dq[0, at, :].astype(jnp.float32)
            outs[j][here, :LANES] = jnp.where(d * code > 0, d, 0.0).astype(jnp.bfloat16)
            code = jnp.where(
                low, block_code(tkv[0, 0, 0, b], skv[0, 0, b]), block_code(tkv[0, 1, 0, b], skv[1, 0, b])
            )
            d = turned[at, :]
            outs[j][here, LANES:] = jnp.where(d * code > 0, d, 0.0).astype(jnp.bfloat16)


def trim_output_body(tasks, place, to, so, do, *outs):
    me = place[0]
    rows, width = outs[0].shape
    low = lax.broadcasted_iota(jnp.int32, (rows, LANES), 1) < BLK
    for j in range(tasks):
        first = (me ^ j) * rows
        at = pl.ds(pl.multiple_of(first, rows), rows)
        b = first // BLK
        for c in range(width // LANES):
            cols = slice(c * LANES, (c + 1) * LANES)
            code = jnp.where(
                low,
                block_code(to[0, b, 2 * c], so[b, 2 * c]),
                block_code(to[0, b, 2 * c + 1], so[b, 2 * c + 1]),
            )
            d = do[0, at, cols].astype(jnp.float32)
            outs[j][:, cols] = jnp.where(d * code > 0, d, 0.0).astype(jnp.bfloat16)


def base_input_body(place, bq, bkv, out, turned):
    transpose_columns(lambda c: keyval_tile(bkv, c), turned)
    rows = out.shape[0]
    at = pl.ds(pl.multiple_of(place[0] * rows, BLK), rows)
    out[:, :LANES] = bq[at, :]
    out[:, LANES:] = turned[at, :].astype(jnp.bfloat16)


def merged(base, parts, gain=1.0):
    total = jnp.zeros(base.shape, jnp.float32)
    count = jnp.zeros(base.shape, jnp.float32)
    for part in parts:
        value = part.astype(jnp.float32)
        total = total + value
        count = count + jnp.where(value != 0, 1.0, 0.0)
    value = base.astype(jnp.float32) + total / jnp.maximum(count, 1.0)
    return (value * gain).astype(jnp.bfloat16)


def merge_input_body(base, *refs):
    out = refs[-1]
    step = BLK
    for r in range(out.shape[0] // step):
        at = slice(r * step, (r + 1) * step)
        out[at, :] = merged(base[at, :], [p[at, :] for p in refs[:-1]])


def merge_output_body(place, gain, base, *refs):
    out = refs[-1]
    rows, width = out.shape
    start = place[1] * width
    at = pl.ds(pl.multiple_of(place[0] * rows, rows), rows)
    step = 4 * LANES
    for c in range(0, width, step):
        cols = slice(c, min(c + step, width))
        size = min(c + step, width) - c
        factor = gain[0:1, pl.ds(pl.multiple_of(start + c, LANES), size)]
        out[:, cols] = merged(base[at, cols], [p[:, cols] for p in refs[:-1]], factor)


def turn(values, cosine, sine):
    return values * cosine + pltpu.roll(values, values.shape[-1] // 2, 1) * sine


def project_body(masks, tasks, place, normed, cosine, sine, *refs):
    pieces, q_out, kv_out = refs[:-2], refs[-2], refs[-1]
    total = jnp.zeros((q_out.shape[0], 2 * LANES), jnp.float32)
    for (tm, dm), piece in zip(masks, pieces):
        block = (place[1] ^ dm) * tasks + (place[0] ^ tm)
        total = total + jnp.dot(normed[block], piece[...], preferred_element_type=jnp.float32)
    q = turn(total[:, :LANES], cosine[...], sine[...])
    q_out[...] = (q * QUERY_SCALE).astype(jnp.bfloat16)
    kv_out[...] = total[:, LANES:].astype(jnp.bfloat16)


def join_body(place, cosine, sine, own, other, out):
    mine, theirs = own[...].astype(jnp.float32), other[...].astype(jnp.float32)
    even = place[2] % 2 == 0
    first = jnp.where(even, mine, theirs)
    second = jnp.where(even, theirs, mine)
    low = lax.broadcasted_iota(jnp.int32, first.shape, 1) < LANES // 2
    keys = jnp.where(low, first, pltpu.roll(second, LANES // 2, 1))
    values = jnp.where(low, pltpu.roll(first, LANES // 2, 1), second)
    out[:, :LANES] = turn(keys, cosine[...], sine[...]).astype(jnp.bfloat16)
    out[:, LANES:] = values.astype(jnp.bfloat16)


def attend_body(masks, halves, place, q_ref, *refs):
    pieces, out = refs[:-1], refs[-1]
    rows = q_ref.shape[0]
    q = q_ref[...]
    mine = place[0] * halves + place[1]
    row = lax.broadcasted_iota(jnp.int32, (rows, rows), 0)
    col = lax.broadcasted_iota(jnp.int32, (rows, rows), 1)
    top = jnp.zeros((rows, LANES), jnp.float32)
    bottom = jnp.zeros((rows, 1), jnp.float32)
    for (tm, dm), piece in zip(masks, pieces):
        theirs = (place[0] ^ tm) * halves + (place[1] ^ dm)
        scores = lax.dot_general(
            q, piece[:, :LANES], (((1,), (1,)), ((), ())), preferred_element_type=jnp.float32
        )
        capped = SCORE_CAP * jnp.tanh(scores / SCORE_CAP)
        allowed = col + theirs * rows <= row + mine * rows
        weights = jnp.where(allowed, jnp.exp(capped), 0.0)
        bottom = bottom + jnp.sum(weights, axis=1, keepdims=True)
        top = top + jnp.dot(
            weights.astype(jnp.bfloat16), piece[:, LANES:], preferred_element_type=jnp.float32
        )
    out[...] = (top / bottom).astype(jnp.bfloat16)


def output_body(masks, place, attention, *refs):
    pieces, out, whole = refs[:-2], refs[-2], refs[-1]
    for (tm, dm), piece in zip(masks, pieces):
        whole[place[1] ^ dm, place[0] ^ tm] = piece[...]
    halves, tasks, rows, width = whole.shape
    for h in range(halves):
        weight = whole[h].reshape(tasks * rows, width)
        out[:, h * width : (h + 1) * width] = jnp.dot(
            attention[...], weight, preferred_element_type=jnp.float32
        ).astype(jnp.bfloat16)


def heads_body(masks, place, *refs):
    parts, out = refs[:-1], refs[-1]
    for m, part in zip(masks, parts):
        out[:, pl.ds(pl.multiple_of((place[2] ^ m) * LANES, LANES), LANES)] = part[...]


def assemble_body(labels, place, *refs):
    pieces, plain = refs[:-1], refs[-1]
    rows, half = plain.shape[2], pieces[0].shape[1]
    for (tm, dm, first), piece in zip(labels, pieces):
        h, t = place[1] ^ dm, place[0] ^ tm
        cols = pl.ds(pl.multiple_of(h * half, LANES), half)
        for m in range(piece.shape[0] // rows):
            plain[place[2] ^ (first + m), t, :, cols] = piece[m * rows : (m + 1) * rows, :]


def statistics_body(attention, weight, hidden, to_plain, to_post, out):
    rows, width = hidden.shape
    step = width // 4
    squares = jnp.zeros((rows, 1), jnp.float32)
    parts = []
    for c in range(0, width, step):
        p = jnp.dot(
            attention[...], weight[:, c : c + step], preferred_element_type=jnp.float32
        )
        plain = p * to_plain[0:1, c : c + step]
        squares = squares + jnp.sum(plain * plain, axis=1, keepdims=True)
        parts.append(p)
    inner = lax.rsqrt(squares / width + EPSILON)
    squares = jnp.zeros((rows, 1), jnp.float32)
    for i, p in enumerate(parts):
        cols = slice(i * step, (i + 1) * step)
        stream = hidden[:, cols].astype(jnp.float32) + p * inner * to_post[0:1, cols]
        squares = squares + jnp.sum(stream * stream, axis=1, keepdims=True)
    outer = lax.rsqrt(squares / width + EPSILON)
    lane = lax.broadcasted_iota(jnp.int32, (rows, LANES), 1)
    table = jnp.where(lane == 0, inner, jnp.where(lane == 1, outer, 0.0))
    out[...] = table.T[: out.shape[0], :]


def contract_body(step, table, *refs):
    left, out, total = refs[:-2], refs[-2], refs[-1]

    def add(k, first):
        cols = pl.ds(pl.multiple_of(k * step, LANES), step)
        rows = [ref[:, cols] for ref in left]
        product = lax.dot_general(
            jnp.concatenate(rows, axis=0) if len(rows) > 1 else rows[0],
            table[:, cols],
            (((1,), (1,)), ((), ())),
            preferred_element_type=jnp.float32,
        )
        total[...] = product if first else total[...] + product

    add(0, True)

    @pl.loop(1, table.shape[1] // step)
    def _(k):
        add(k, False)

    out[...] = total[...].astype(out.dtype)


def contract(left, table, dtype):
    width = table.shape[1]
    step = width // 4 if width % (4 * LANES) == 0 else width
    rows = sum(block.shape[0] for block in left)
    vocab = table.shape[0]
    return pl.pallas_call(
        functools.partial(contract_body, step),
        out_shape=shape_of((rows, vocab), dtype),
        in_specs=[VMEM] * (1 + len(left)),
        out_specs=VMEM,
        scratch_shapes=[pltpu.VMEM((rows, vocab), jnp.float32)],
        compiler_params=pltpu.CompilerParams(vmem_limit_bytes=CONTRACT_VMEM),
        cost_estimate=pl.CostEstimate(
            flops=2 * rows * width * vocab,
            bytes_accessed=2 * (rows + vocab) * width + 4 * rows * vocab,
            transcendentals=0,
        ),
    )(table, *left)


def score_body(masks, halves, shares, place, targets, mixed, *refs):
    count = len(masks)
    attention, stats = refs[:count], refs[count : 2 * count]
    first, early, late, out = refs[2 * count :]
    rows = attention[0].shape[0]
    cut = rows // 2
    share = rows // shares
    vocab = mixed.shape[1]
    first_id = place[3]
    z = place[2]
    side = z // (shares // 2)
    lane = lax.broadcasted_iota(jnp.int32, (rows, LANES), 1)
    late_rows = cut + rows + cut

    def halves_of(mine, rest):
        top = jnp.where(side == 0, mine, rest)
        bottom = jnp.where(side == 0, rest, mine)
        return jnp.concatenate([top, bottom], axis=0)

    def by_share(start, natural, cols):
        found = []
        for s in natural:
            at = pl.multiple_of(start + (z ^ s) * share, share)
            found.append(late[pl.ds(at, share), cols])
        return jnp.concatenate(found, axis=0)

    for n, (tm, dm) in enumerate(masks):
        group = (place[0] ^ tm) * halves + (place[1] ^ dm)
        table = stats[n][...].T
        wanted = jnp.broadcast_to(targets[pl.ds(group, 1), :], (8, rows)).T
        inner, outer, wanted = table[:, 0:1], table[:, 1:2], wanted[:, 0:1]
        core = tm % 2
        own = core * rows
        far = core * late_rows
        sums = jnp.zeros((rows, LANES), jnp.float32)
        hits = jnp.zeros((rows, LANES), jnp.float32)
        product = jnp.dot(attention[n][...], mixed[...], preferred_element_type=jnp.float32)
        for v in range(vocab // LANES):
            cols = slice(v * LANES, (v + 1) * LANES)
            if tm < 2 and not dm:
                plain = first[own : own + rows, cols]
            elif tm < 2:
                plain = halves_of(early[own : own + cut, cols], early[own + cut : own + rows, cols])
            elif not dm:
                plain = by_share(far + cut, range(shares), cols)
            else:
                count_rest = shares // 2
                rest = by_share(
                    far + rows,
                    [(1 - side) * count_rest + i for i in range(count_rest)],
                    cols,
                )
                plain = halves_of(late[far : far + cut, cols], rest)
            logits = outer * (plain + inner * product[:, cols])
            capped = LOGIT_CAP * jnp.tanh(logits / LOGIT_CAP)
            sums = sums + jnp.exp(capped)
            hits = hits + jnp.where(lane + (first_id + v * LANES) == wanted, capped, 0.0)
        for kind, value in ((0, sums), (1, hits)):
            out[kind, pl.ds(group, 1), :] = jnp.sum(value.T, axis=0, keepdims=True)


def loss_body(halves, place, mask, first, second, own, summary):
    both = first[...] + second[...]
    counted = mask[...].astype(jnp.float32)
    losses = (jnp.log(both[0]) - both[1]) * counted
    at = pl.ds(place[0] * halves + place[1], 1)
    sumexp = first[0, at, :] + second[0, at, :]
    target = first[1, at, :] + second[1, at, :]
    own[...] = (jnp.log(sumexp) - target) * mask[at, :].astype(jnp.float32)
    summary[0] = jnp.sum(losses)
    summary[1] = jnp.sum(counted)


def rms_norm(values, gain):
    scale = lax.rsqrt(jnp.mean(values * values, axis=-1, keepdims=True) + EPSILON)
    return values * scale * gain


def general_tail(
    place, masks, attention, piece_out, hidden, post_gain, final_gain, unembedding, targets, loss_mask
):
    bf16, f32 = jnp.bfloat16, jnp.float32
    tasks = lax.axis_size(TASK)
    tensors = lax.axis_size(TENSOR)
    halves = lax.axis_size(DP)
    task, dp, tensor = lax.axis_index(TASK), lax.axis_index(DP), lax.axis_index(TENSOR)
    row_count, width = hidden.shape
    out_rows, half = piece_out.shape
    residual = hidden.astype(f32)
    group_index = task * halves + dp
    pieces_out = gather_group(piece_out)
    partial_value = kernel_call(
        functools.partial(output_body, masks),
        [place, attention] + [b for _, _, b in pieces_out],
        [SMEM] + [VMEM] * (1 + len(masks)),
        [shape_of((row_count, width), bf16)],
        [pltpu.VMEM((halves, tasks, out_rows, half), bf16)],
        flops=2 * row_count * width * LANES,
    )[0]

    span_rows = row_count // tensors
    share_rows = lax.psum_scatter(partial_value, TENSOR, scatter_dimension=0, tiled=True).astype(f32)
    own_stream = lax.dynamic_slice_in_dim(residual, tensor * span_rows, span_rows, 0)
    stream = own_stream + rms_norm(share_rows, post_gain)
    final = rms_norm(stream, final_gain).astype(bf16)
    every_rows = lax.all_gather(final, (TASK, TENSOR, DP), axis=0, tiled=True)

    def order(values):
        return jnp.transpose(
            values.reshape(tasks, halves, tensors, span_rows), (0, 2, 1, 3)
        ).reshape(-1)

    ordered_targets, ordered_mask = order(targets), order(loss_mask)
    logits = lax.dot_general(
        every_rows, unembedding, (((1,), (1,)), ((), ())), preferred_element_type=f32
    )
    capped = LOGIT_CAP * jnp.tanh(logits / LOGIT_CAP)
    vocab_ids = lax.axis_index((TASK, TENSOR, DP)) * unembedding.shape[0] + jnp.arange(
        unembedding.shape[0], dtype=jnp.int32
    )
    local_sumexp = jnp.sum(jnp.exp(capped), axis=1)
    local_target = jnp.sum(
        jnp.where(ordered_targets[:, None] == vocab_ids[None, :], capped, 0.0), axis=1
    )
    both = jnp.stack([local_sumexp, local_target])
    both = total_over_group(total_over(both, TENSOR))
    sumexp, target_logit = both[0], both[1]
    counted = ordered_mask.astype(f32)
    losses = (jnp.log(sumexp) - target_logit) * counted
    summary = jnp.stack([jnp.sum(losses), jnp.sum(counted)])
    losses = jnp.transpose(
        losses.reshape(tasks, tensors, halves, span_rows), (0, 2, 1, 3)
    ).reshape(-1)
    own_losses = lax.dynamic_slice_in_dim(losses, group_index * row_count, row_count, 0)
    return (own_losses, summary)


def paired(blocks):
    return blocks + [swap(block, TASK, 1) for block in blocks]


def send_hidden(hidden, kept, tensor):
    tensors = lax.axis_size(TENSOR)
    rows = hidden.shape[0] // tensors
    cut = hidden.shape[0] // 2
    hidden = after([hidden], [kept])[0]
    side = tensor // (tensors // 2)
    share = lax.dynamic_slice_in_dim(hidden, tensor * rows, rows, 0)
    mine = lax.dynamic_slice_in_dim(hidden, side * cut, cut, 0)
    rest = lax.dynamic_slice_in_dim(hidden, (1 - side) * cut, cut, 0)
    dp_mine = swap(mine, DP, 1)
    by_task = swap(share, TASK, 2)
    dp_rest = swap(rest, DP, 1)
    both_mine = swap(dp_mine, TASK, 2)
    shares = [by_task] + [swap(by_task, TENSOR, m) for m in range(1, tensors)]
    both_rest = [swap(shares[m], DP, 1) for m in range(tensors // 2, tensors)]
    return [hidden, dp_mine, dp_rest], [both_mine], shares + both_rest


def split_tail(
    where,
    attention,
    piece_out,
    inverse_gains,
    late_rows,
    base,
    hidden,
    unembedding,
    targets,
    loss_mask,
):
    bf16, f32 = jnp.bfloat16, jnp.float32
    tasks = lax.axis_size(TASK)
    tensors = lax.axis_size(TENSOR)
    halves = lax.axis_size(DP)
    row_count, width = hidden.shape
    out_rows, _ = piece_out.shape
    groups = tasks * halves
    vocab = unembedding.shape[0]
    place = where
    to_plain, to_post = inverse_gains

    features = tensors * tasks * out_rows
    received = after([swap(attention, TENSOR, m) for m in range(1, tensors)], base[1:])
    heads = kernel_call(
        functools.partial(heads_body, list(range(tensors))),
        [place, attention] + received,
        [SMEM] + [VMEM] * tensors,
        [shape_of((row_count, features), bf16)],
    )[0]
    late = contract(paired(after(late_rows, [attention])), unembedding, f32)
    column = jnp.concatenate([piece_out] + [swap(piece_out, TENSOR, m) for m in range(1, tensors)], axis=0)
    by_task, by_dp = swap(column, TASK, 2), swap(column, DP, 1)
    cut = column.shape[0] // 2
    parts = [
        (0, 0, 0, column),
        (2, 0, 0, by_task),
        (0, 1, 0, by_dp),
        (2, 1, 0, swap(by_dp[:cut], TASK, 2)),
        (2, 1, cut // out_rows, swap(by_task[cut:], DP, 1)),
    ]
    parts += [(tm ^ 1, dm, first, swap(b, TASK, 1)) for tm, dm, first, b in parts]
    tied = after([part[3] for part in parts[3:5]], [late])
    parts[3:5] = [part[:3] + (block,) for part, block in zip(parts[3:5], tied)]
    plain = kernel_call(
        functools.partial(assemble_body, [part[:3] for part in parts]),
        [place] + [part[3] for part in parts],
        [SMEM] + [VMEM] * len(parts),
        [shape_of((tensors, tasks, out_rows, width), bf16)],
    )[0]
    plain = plain.reshape(features, width)
    mixed = contract([plain], unembedding, bf16)

    stats = kernel_call(
        statistics_body,
        [heads, plain, hidden, to_plain, to_post],
        [VMEM] * 5,
        [shape_of((8, row_count), f32)],
        flops=2 * row_count * features * width,
    )[0]
    every_heads = gather_group(heads)
    every_stats = gather_group(stats)
    both = kernel_call(
        functools.partial(score_body, [(tm, dm) for tm, dm, _ in every_heads], halves, tensors),
        [where, targets.reshape(groups, row_count), mixed]
        + [b for _, _, b in every_heads]
        + [b for _, _, b in every_stats]
        + base + [late],
        [SMEM] + [VMEM] * (5 + 2 * groups),
        [shape_of((2, groups, row_count), f32)],
        flops=2 * groups * row_count * features * vocab,
        transcendentals=2 * groups * row_count * vocab,
    )[0]
    both = total_over(both, TENSOR)
    parts = [swap_two(both, tm, dm) for tm in range(0, tasks, 2) for dm in range(halves) if tm or dm]
    for part in parts:
        both = both + part
    own, summary = pl.pallas_call(
        functools.partial(loss_body, halves),
        out_shape=[shape_of((1, row_count), f32), shape_of((2,), f32)],
        in_specs=[SMEM] + [VMEM] * 3,
        out_specs=[VMEM, SMEM],
        name="loss",
    )(place, loss_mask.reshape(groups, row_count), both, swap(both, TASK, 1))
    return own.reshape(row_count), summary


def on_device(
    hidden,
    pre_gain,
    base_query,
    base_keyval,
    base_output,
    delta_query,
    delta_keyval,
    delta_output,
    trim_query,
    trim_keyval,
    trim_output,
    sign_query,
    sign_keyval,
    sign_output,
    post_gain,
    final_gain,
    unembedding,
    targets,
    loss_mask,
):
    bf16, f32 = jnp.bfloat16, jnp.float32
    tasks = lax.axis_size(TASK)
    tensors = lax.axis_size(TENSOR)
    halves = lax.axis_size(DP)
    task, dp, tensor = lax.axis_index(TASK), lax.axis_index(DP), lax.axis_index(TENSOR)
    place = jnp.stack([task, dp, tensor]).astype(jnp.int32)
    row_count, width = hidden.shape
    half = base_query.shape[0]
    quarter = half // tasks
    out_rows = base_output.shape[0] // tasks

    kept_in = kernel_call(
        functools.partial(trim_input_body, tasks),
        [
            place,
            jnp.swapaxes(trim_query, 1, 2),
            jnp.swapaxes(trim_keyval, 2, 3),
            sign_query.T,
            jnp.swapaxes(sign_keyval, 1, 2),
            delta_query,
            jnp.swapaxes(delta_keyval, 2, 3),
        ],
        [SMEM] * 5 + [VMEM] * 2,
        [shape_of((quarter, 2 * LANES), bf16)] * tasks,
        [pltpu.VMEM((half, LANES), f32)],
    )
    got_in = [kept_in[0]] + [swap(kept_in[j], TASK, j) for j in range(1, tasks)]
    kept_out = kernel_call(
        functools.partial(trim_output_body, tasks),
        [place, trim_output, sign_output, delta_output],
        [SMEM] * 3 + [VMEM],
        [shape_of((out_rows, half), bf16)] * tasks,
    )
    base_in = kernel_call(
        base_input_body,
        [place, base_query, jnp.swapaxes(base_keyval, 1, 2)],
        [SMEM] + [VMEM] * 2,
        [shape_of((quarter, 2 * LANES), bf16)],
        [pltpu.VMEM((half, LANES), f32)],
    )[0]

    early_hidden, early_place = after([hidden, place], [kept_in[0]])
    normed = rms_norm(early_hidden.astype(f32), pre_gain).astype(bf16)
    blocks = width // quarter
    normed = jnp.transpose(normed.reshape(row_count, blocks, quarter), (1, 0, 2))
    group_index = early_place[0] * halves + early_place[1]
    query_positions = group_index * row_count + jnp.arange(row_count, dtype=jnp.int32)
    half_head = LANES // 2
    frequencies = jnp.exp(
        -jnp.log(ROPE_BASE) * 2.0 * jnp.arange(half_head, dtype=jnp.int32).astype(f32) / LANES
    )
    angles = query_positions.astype(f32)[:, None] * frequencies[None, :]
    cosine, sine = jnp.cos(angles), jnp.sin(angles)
    cosine = jnp.concatenate([cosine, cosine], axis=1)
    sine = jnp.concatenate([-sine, sine], axis=1)

    gathered_bytes = tensors * base_output.shape[0] * width * base_output.dtype.itemsize
    low_rank = gathered_bytes <= 6 * 2**20 and tensors in (2, 4)
    where = jnp.concatenate(
        [place, (lax.axis_index((TASK, TENSOR, DP)) * unembedding.shape[0]).astype(jnp.int32)[None]]
    )
    if low_rank:
        weight_gain = (post_gain * final_gain)[None, :]
        rows = [weight_gain, 1.0 / weight_gain, (1.0 / final_gain)[None, :], where]
    else:
        rows = [jnp.ones((1, width), f32), where]
    tied = after(list(got_in) + rows, [normed, cosine, sine])
    got_in, rows = tied[:tasks], tied[tasks:]
    weight_gain, where = rows[0], rows[-1]
    piece_in = kernel_call(
        merge_input_body,
        [base_in] + got_in,
        [VMEM] * (1 + tasks),
        [shape_of((quarter, 2 * LANES), bf16)],
    )[0]
    pieces_in = gather_group(piece_in)
    masks = [(tm, dm) for tm, dm, _ in pieces_in]

    kept_out = after(kept_out, [piece_in])
    got_out = [kept_out[0]] + [swap(kept_out[j], TASK, j) for j in range(1, tasks)]
    got_out = after(got_out, [b for _, _, b in pieces_in[1:4]])
    if low_rank:
        scaled = (hidden.astype(f32) * final_gain).astype(bf16)
        early_rows, middle_rows, late_rows = send_hidden(scaled, kept_in[0], tensor)
        base = [contract(paired(early_rows[:1]), unembedding, f32)]
        base.append(contract(paired(early_rows[1:]), unembedding, f32))
    piece_out = kernel_call(
        merge_output_body,
        [place, weight_gain, base_output] + got_out,
        [SMEM] + [VMEM] * (2 + tasks),
        [shape_of((out_rows, half), bf16)],
    )[0]

    queries, keyval = kernel_call(
        functools.partial(project_body, masks, tasks),
        [place, normed, cosine, sine] + [b for _, _, b in pieces_in],
        [SMEM] + [VMEM] * (3 + len(masks)),
        [shape_of((row_count, LANES), bf16)] * 2,
        flops=2 * row_count * width * 2 * LANES,
    )
    other = swap(keyval, TENSOR, 1)
    joined = kernel_call(
        join_body,
        [place, cosine, sine, keyval, other],
        [SMEM] + [VMEM] * 4,
        [shape_of((row_count, 2 * LANES), bf16)],
    )[0]
    every_keyval = gather_group(joined)
    attention = kernel_call(
        functools.partial(attend_body, masks, halves),
        [place, queries] + [b for _, _, b in every_keyval],
        [SMEM] + [VMEM] * (1 + len(masks)),
        [shape_of((row_count, LANES), bf16)],
        flops=4 * row_count * row_count * LANES * len(masks),
        transcendentals=2 * row_count * row_count * len(masks),
    )[0]
    if not low_rank:
        return general_tail(
            place, masks, attention, piece_out, hidden, post_gain, final_gain, unembedding, targets, loss_mask
        )
    return split_tail(
        where,
        attention,
        piece_out,
        rows[1:3],
        middle_rows + late_rows,
        base,
        hidden,
        unembedding,
        targets,
        loss_mask,
    )


def solution(mesh):
    return jax.shard_map(
        on_device,
        mesh=mesh,
        in_specs=(
            P((TASK, DP), None),
            P(),
            P(DP, TENSOR),
            P(None, DP, TENSOR),
            P(TENSOR, DP),
            P(TASK, DP, TENSOR),
            P(TASK, None, DP, TENSOR),
            P(TASK, TENSOR, DP),
            P(TASK, DP, TENSOR),
            P(TASK, None, DP, TENSOR),
            P(TASK, TENSOR, DP),
            P(DP, TENSOR),
            P(None, DP, TENSOR),
            P(TENSOR, DP),
            P(),
            P(),
            P((TASK, TENSOR, DP), None),
            P(),
            P(),
        ),
        out_specs=(P((TASK, DP)), P()),
        check_vma=False,
    )
```

```python
import functools

import jax
import jax.numpy as jnp
from jax import lax
from jax.experimental import pallas as pl
from jax.experimental.pallas import tpu as pltpu
from jax.sharding import PartitionSpec as P


TASK, TENSOR, DP = "task", "tensor", "dp"

BLK = 64
LANES = 128

EPSILON = 1e-06
QUERY_SCALE = 1.0 / 12.0
ROPE_BASE = 10000.0
SCORE_CAP = 50.0
LOGIT_CAP = 30.0


KERNEL_VMEM = 20 * 2**20
CONTRACT_VMEM = 28 * 2**20

VMEM = pl.BlockSpec(memory_space=pltpu.VMEM)
SMEM = pl.BlockSpec(memory_space=pltpu.SMEM)


def kernel_call(body, inputs, in_specs, outputs, scratch=(), flops=1, transcendentals=0, grant=None):
    moved = sum(a.size * a.dtype.itemsize for a in inputs)
    moved += sum(int(jnp.dtype(o.dtype).itemsize) * o.size for o in outputs)
    return pl.pallas_call(
        body,
        out_shape=outputs,
        in_specs=in_specs,
        out_specs=[VMEM] * len(outputs),
        scratch_shapes=list(scratch),
        compiler_params=pltpu.CompilerParams(vmem_limit_bytes=grant or KERNEL_VMEM),
        cost_estimate=pl.CostEstimate(
            flops=flops, bytes_accessed=moved, transcendentals=transcendentals
        ),
    )(*inputs)


def shape_of(dims, dtype):
    return jax.ShapeDtypeStruct(tuple(dims), dtype)


def swap(block, axis, mask):
    count = lax.axis_size(axis)
    return lax.ppermute(block, axis, [(i, i ^ mask) for i in range(count)])


def swap_two(block, task_mask, dp_mask):
    tasks, halves = lax.axis_size(TASK), lax.axis_size(DP)
    route = []
    for t in range(tasks):
        for d in range(halves):
            route.append((t * halves + d, (t ^ task_mask) * halves + (d ^ dp_mask)))
    return lax.ppermute(block, (TASK, DP), route)


def gather_group(block):
    tasks, halves = lax.axis_size(TASK), lax.axis_size(DP)
    near = [(0, 0, block)]
    for tm in range(0, tasks, 2):
        for dm in range(halves):
            if tm or dm:
                if not dm:
                    got = swap(block, TASK, tm)
                elif not tm:
                    got = swap(block, DP, dm)
                else:
                    got = swap_two(block, tm, dm)
                near.append((tm, dm, got))
    return near + [(tm ^ 1, dm, swap(b, TASK, 1)) for tm, dm, b in near]


def after(values, earlier):
    count = len(values)
    return list(lax.optimization_barrier(tuple(values) + tuple(earlier))[:count])


def total_over(value, axis):
    count = lax.axis_size(axis)
    if count <= 4:
        parts = [swap(value, axis, m) for m in range(1, count)]
        for part in parts:
            value = value + part
        return value
    step = 1
    while step < count:
        value = value + swap(value, axis, step)
        step *= 2
    return value


def total_over_group(value):
    tasks, halves = lax.axis_size(TASK), lax.axis_size(DP)
    parts = []
    for tm in range(0, tasks, 2):
        for dm in range(halves):
            if tm or dm:
                parts.append(swap_two(value, tm, dm))
    for part in parts:
        value = value + part
    return value + swap(value, TASK, 1)


def block_code(trim, sign):
    return (trim * (2 * sign - 1)).astype(jnp.float32)


def transpose_columns(source, out_ref):
    for c in range(out_ref.shape[0] // LANES):
        out_ref[c * LANES : (c + 1) * LANES, :] = source(c).astype(jnp.float32).T


def keyval_tile(ref, c):
    both = ref[:, :, c * LANES : (c + 1) * LANES]
    return both.reshape(2 * both.shape[1], LANES)


def trim_input_body(tasks, place, tq, tkv, sq, skv, dq, dkv, *rest):
    outs, turned = rest[:-1], rest[-1]
    me = place[0]
    transpose_columns(lambda c: keyval_tile(dkv.at[0], c), turned)
    rows = outs[0].shape[0]
    blocks = rows // BLK
    low = lax.broadcasted_iota(jnp.int32, (BLK, LANES), 1) < BLK
    for j in range(tasks):
        first = (me ^ j) * blocks
        for r in range(blocks):
            b = first + r
            at = pl.ds(pl.multiple_of(b * BLK, BLK), BLK)
            here = slice(r * BLK, (r + 1) * BLK)
            code = jnp.where(
                low, block_code(tq[0, 0, b], sq[0, b]), block_code(tq[0, 1, b], sq[1, b])
            )
            d = dq[0, at, :].astype(jnp.float32)
            outs[j][here, :LANES] = jnp.where(d * code > 0, d, 0.0).astype(jnp.bfloat16)
            code = jnp.where(
                low, block_code(tkv[0, 0, 0, b], skv[0, 0, b]), block_code(tkv[0, 1, 0, b], skv[1, 0, b])
            )
            d = turned[at, :]
            outs[j][here, LANES:] = jnp.where(d * code > 0, d, 0.0).astype(jnp.bfloat16)


def trim_output_body(tasks, place, to, so, do, *outs):
    me = place[0]
    rows, width = outs[0].shape
    low = lax.broadcasted_iota(jnp.int32, (rows, LANES), 1) < BLK
    for j in range(tasks):
        first = (me ^ j) * rows
        at = pl.ds(pl.multiple_of(first, rows), rows)
        b = first // BLK
        for c in range(width // LANES):
            cols = slice(c * LANES, (c + 1) * LANES)
            code = jnp.where(
                low,
                block_code(to[0, b, 2 * c], so[b, 2 * c]),
                block_code(to[0, b, 2 * c + 1], so[b, 2 * c + 1]),
            )
            d = do[0, at, cols].astype(jnp.float32)
            outs[j][:, cols] = jnp.where(d * code > 0, d, 0.0).astype(jnp.bfloat16)


def prepare_body(hidden, before, last, blocks, scaled):
    x = hidden[...].astype(jnp.float32)
    _, width = x.shape
    scale = lax.rsqrt(jnp.sum(x * x, axis=1, keepdims=True) / width + EPSILON)
    normed = (x * scale * before[...]).astype(jnp.bfloat16)
    step = blocks.shape[2]
    for b in range(blocks.shape[0]):
        blocks[b] = normed[:, b * step : (b + 1) * step]
    scaled[...] = (x * last[...]).astype(jnp.bfloat16)


def base_input_body(place, bq, bkv, out, turned):
    transpose_columns(lambda c: keyval_tile(bkv, c), turned)
    rows = out.shape[0]
    at = pl.ds(pl.multiple_of(place[0] * rows, BLK), rows)
    out[:, :LANES] = bq[at, :]
    out[:, LANES:] = turned[at, :].astype(jnp.bfloat16)


def merged(base, parts, gain=1.0):
    total = jnp.zeros(base.shape, jnp.float32)
    count = jnp.zeros(base.shape, jnp.float32)
    for part in parts:
        value = part.astype(jnp.float32)
        total = total + value
        count = count + jnp.where(value != 0, 1.0, 0.0)
    value = base.astype(jnp.float32) + total / jnp.maximum(count, 1.0)
    return (value * gain).astype(jnp.bfloat16)


def merge_input_body(base, *refs):
    out = refs[-1]
    step = BLK
    for r in range(out.shape[0] // step):
        at = slice(r * step, (r + 1) * step)
        out[at, :] = merged(base[at, :], [p[at, :] for p in refs[:-1]])


def merge_output_body(place, gain, base, *refs):
    out = refs[-1]
    rows, width = out.shape
    start = place[1] * width
    at = pl.ds(pl.multiple_of(place[0] * rows, rows), rows)
    step = 4 * LANES
    for c in range(0, width, step):
        cols = slice(c, min(c + step, width))
        size = min(c + step, width) - c
        factor = gain[0:1, pl.ds(pl.multiple_of(start + c, LANES), size)]
        out[:, cols] = merged(base[at, cols], [p[:, cols] for p in refs[:-1]], factor)


def turn(values, cosine, sine):
    return values * cosine + pltpu.roll(values, values.shape[-1] // 2, 1) * sine


def project_body(masks, tasks, place, normed, cosine, sine, *refs):
    pieces, q_out, kv_out = refs[:-2], refs[-2], refs[-1]
    total = jnp.zeros((q_out.shape[0], 2 * LANES), jnp.float32)
    for (tm, dm), piece in zip(masks, pieces):
        block = (place[1] ^ dm) * tasks + (place[0] ^ tm)
        total = total + jnp.dot(normed[block], piece[...], preferred_element_type=jnp.float32)
    q = turn(total[:, :LANES], cosine[...], sine[...])
    q_out[...] = (q * QUERY_SCALE).astype(jnp.bfloat16)
    kv_out[...] = total[:, LANES:].astype(jnp.bfloat16)


def join_body(place, cosine, sine, own, other, out):
    mine, theirs = own[...].astype(jnp.float32), other[...].astype(jnp.float32)
    even = place[2] % 2 == 0
    first = jnp.where(even, mine, theirs)
    second = jnp.where(even, theirs, mine)
    low = lax.broadcasted_iota(jnp.int32, first.shape, 1) < LANES // 2
    keys = jnp.where(low, first, pltpu.roll(second, LANES // 2, 1))
    values = jnp.where(low, pltpu.roll(first, LANES // 2, 1), second)
    out[:, :LANES] = turn(keys, cosine[...], sine[...]).astype(jnp.bfloat16)
    out[:, LANES:] = values.astype(jnp.bfloat16)


def attend_body(masks, halves, place, q_ref, *refs):
    pieces, out = refs[:-1], refs[-1]
    rows = q_ref.shape[0]
    q = q_ref[...]
    mine = place[0] * halves + place[1]
    row = lax.broadcasted_iota(jnp.int32, (rows, rows), 0)
    col = lax.broadcasted_iota(jnp.int32, (rows, rows), 1)
    top = jnp.zeros((rows, LANES), jnp.float32)
    bottom = jnp.zeros((rows, 1), jnp.float32)
    for (tm, dm), piece in zip(masks, pieces):
        theirs = (place[0] ^ tm) * halves + (place[1] ^ dm)
        scores = lax.dot_general(
            q, piece[:, :LANES], (((1,), (1,)), ((), ())), preferred_element_type=jnp.float32
        )
        capped = SCORE_CAP * jnp.tanh(scores / SCORE_CAP)
        allowed = col + theirs * rows <= row + mine * rows
        weights = jnp.where(allowed, jnp.exp(capped), 0.0)
        bottom = bottom + jnp.sum(weights, axis=1, keepdims=True)
        top = top + jnp.dot(
            weights.astype(jnp.bfloat16), piece[:, LANES:], preferred_element_type=jnp.float32
        )
    out[...] = (top / bottom).astype(jnp.bfloat16)


def output_body(masks, place, attention, *refs):
    pieces, out, whole = refs[:-2], refs[-2], refs[-1]
    for (tm, dm), piece in zip(masks, pieces):
        whole[place[1] ^ dm, place[0] ^ tm] = piece[...]
    halves, tasks, rows, width = whole.shape
    for h in range(halves):
        weight = whole[h].reshape(tasks * rows, width)
        out[:, h * width : (h + 1) * width] = jnp.dot(
            attention[...], weight, preferred_element_type=jnp.float32
        ).astype(jnp.bfloat16)


def heads_body(masks, place, *refs):
    parts, out = refs[:-1], refs[-1]
    for m, part in zip(masks, parts):
        out[:, pl.ds(pl.multiple_of((place[2] ^ m) * LANES, LANES), LANES)] = part[...]


def assemble_body(labels, place, *refs):
    pieces, plain = refs[:-1], refs[-1]
    rows, half = plain.shape[2], pieces[0].shape[1]
    for (tm, dm, first), piece in zip(labels, pieces):
        h, t = place[1] ^ dm, place[0] ^ tm
        cols = pl.ds(pl.multiple_of(h * half, LANES), half)
        for m in range(piece.shape[0] // rows):
            plain[place[2] ^ (first + m), t, :, cols] = piece[m * rows : (m + 1) * rows, :]


def statistics_body(attention, weight, hidden, to_plain, to_post, out):
    rows, width = hidden.shape
    step = width // 4
    squares = jnp.zeros((rows, 1), jnp.float32)
    parts = []
    for c in range(0, width, step):
        p = jnp.dot(
            attention[...], weight[:, c : c + step], preferred_element_type=jnp.float32
        )
        plain = p * to_plain[0:1, c : c + step]
        squares = squares + jnp.sum(plain * plain, axis=1, keepdims=True)
        parts.append(p)
    inner = lax.rsqrt(squares / width + EPSILON)
    squares = jnp.zeros((rows, 1), jnp.float32)
    for i, p in enumerate(parts):
        cols = slice(i * step, (i + 1) * step)
        stream = hidden[:, cols].astype(jnp.float32) + p * inner * to_post[0:1, cols]
        squares = squares + jnp.sum(stream * stream, axis=1, keepdims=True)
    outer = lax.rsqrt(squares / width + EPSILON)
    lane = lax.broadcasted_iota(jnp.int32, (rows, LANES), 1)
    table = jnp.where(lane == 0, inner, jnp.where(lane == 1, outer, 0.0))
    out[...] = table.T[: out.shape[0], :]


def contract_body(step, table, *refs):
    left, out, total = refs[:-2], refs[-2], refs[-1]

    def add(k, first):
        cols = pl.ds(pl.multiple_of(k * step, LANES), step)
        rows = [ref[:, cols] for ref in left]
        product = lax.dot_general(
            jnp.concatenate(rows, axis=0) if len(rows) > 1 else rows[0],
            table[:, cols],
            (((1,), (1,)), ((), ())),
            preferred_element_type=jnp.float32,
        )
        total[...] = product if first else total[...] + product

    add(0, True)

    @pl.loop(1, table.shape[1] // step)
    def _(k):
        add(k, False)

    out[...] = total[...].astype(out.dtype)


def contract(left, table, dtype):
    width = table.shape[1]
    step = width // 4 if width % (4 * LANES) == 0 else width
    rows = sum(block.shape[0] for block in left)
    vocab = table.shape[0]
    return pl.pallas_call(
        functools.partial(contract_body, step),
        out_shape=shape_of((rows, vocab), dtype),
        in_specs=[VMEM] * (1 + len(left)),
        out_specs=VMEM,
        scratch_shapes=[pltpu.VMEM((rows, vocab), jnp.float32)],
        compiler_params=pltpu.CompilerParams(vmem_limit_bytes=CONTRACT_VMEM),
        cost_estimate=pl.CostEstimate(
            flops=2 * rows * width * vocab,
            bytes_accessed=2 * (rows + vocab) * width + 4 * rows * vocab,
            transcendentals=0,
        ),
    )(table, *left)


def score_body(masks, halves, shares, place, targets, mixed, *refs):
    count = len(masks)
    attention, stats = refs[:count], refs[count : 2 * count]
    first, early, late, out = refs[2 * count :]
    rows = attention[0].shape[0]
    cut = rows // 2
    share = rows // shares
    vocab = mixed.shape[1]
    first_id = place[3]
    z = place[2]
    side = z // (shares // 2)
    lane = lax.broadcasted_iota(jnp.int32, (rows, LANES), 1)
    late_rows = cut + rows + cut

    def halves_of(mine, rest):
        top = jnp.where(side == 0, mine, rest)
        bottom = jnp.where(side == 0, rest, mine)
        return jnp.concatenate([top, bottom], axis=0)

    def by_share(start, natural, cols):
        found = []
        for s in natural:
            at = pl.multiple_of(start + (z ^ s) * share, share)
            found.append(late[pl.ds(at, share), cols])
        return jnp.concatenate(found, axis=0)

    for n, (tm, dm) in enumerate(masks):
        group = (place[0] ^ tm) * halves + (place[1] ^ dm)
        table = stats[n][...].T
        wanted = jnp.broadcast_to(targets[pl.ds(group, 1), :], (8, rows)).T
        inner, outer, wanted = table[:, 0:1], table[:, 1:2], wanted[:, 0:1]
        core = tm % 2
        own = core * rows
        far = core * late_rows
        sums = jnp.zeros((rows, LANES), jnp.float32)
        hits = jnp.zeros((rows, LANES), jnp.float32)
        product = jnp.dot(attention[n][...], mixed[...], preferred_element_type=jnp.float32)
        for v in range(vocab // LANES):
            cols = slice(v * LANES, (v + 1) * LANES)
            if tm < 2 and not dm:
                plain = first[own : own + rows, cols]
            elif tm < 2:
                plain = halves_of(early[own : own + cut, cols], early[own + cut : own + rows, cols])
            elif not dm:
                plain = by_share(far + cut, range(shares), cols)
            else:
                count_rest = shares // 2
                rest = by_share(
                    far + rows,
                    [(1 - side) * count_rest + i for i in range(count_rest)],
                    cols,
                )
                plain = halves_of(late[far : far + cut, cols], rest)
            logits = outer * (plain + inner * product[:, cols])
            capped = LOGIT_CAP * jnp.tanh(logits / LOGIT_CAP)
            sums = sums + jnp.exp(capped)
            hits = hits + jnp.where(lane + (first_id + v * LANES) == wanted, capped, 0.0)
        for kind, value in ((0, sums), (1, hits)):
            out[kind, pl.ds(group, 1), :] = jnp.sum(value.T, axis=0, keepdims=True)


def loss_body(halves, place, mask, first, second, own, summary):
    both = first[...] + second[...]
    counted = mask[...].astype(jnp.float32)
    losses = (jnp.log(both[0]) - both[1]) * counted
    at = pl.ds(place[0] * halves + place[1], 1)
    sumexp = first[0, at, :] + second[0, at, :]
    target = first[1, at, :] + second[1, at, :]
    own[...] = (jnp.log(sumexp) - target) * mask[at, :].astype(jnp.float32)
    summary[0] = jnp.sum(losses)
    summary[1] = jnp.sum(counted)


def rms_norm(values, gain):
    scale = lax.rsqrt(jnp.mean(values * values, axis=-1, keepdims=True) + EPSILON)
    return values * scale * gain


def general_tail(
    place, masks, attention, piece_out, hidden, post_gain, final_gain, unembedding, targets, loss_mask
):
    bf16, f32 = jnp.bfloat16, jnp.float32
    tasks = lax.axis_size(TASK)
    tensors = lax.axis_size(TENSOR)
    halves = lax.axis_size(DP)
    task, dp, tensor = lax.axis_index(TASK), lax.axis_index(DP), lax.axis_index(TENSOR)
    row_count, width = hidden.shape
    out_rows, half = piece_out.shape
    residual = hidden.astype(f32)
    group_index = task * halves + dp
    pieces_out = gather_group(piece_out)
    partial_value = kernel_call(
        functools.partial(output_body, masks),
        [place, attention] + [b for _, _, b in pieces_out],
        [SMEM] + [VMEM] * (1 + len(masks)),
        [shape_of((row_count, width), bf16)],
        [pltpu.VMEM((halves, tasks, out_rows, half), bf16)],
        flops=2 * row_count * width * LANES,
    )[0]

    span_rows = row_count // tensors
    share_rows = lax.psum_scatter(partial_value, TENSOR, scatter_dimension=0, tiled=True).astype(f32)
    own_stream = lax.dynamic_slice_in_dim(residual, tensor * span_rows, span_rows, 0)
    stream = own_stream + rms_norm(share_rows, post_gain)
    final = rms_norm(stream, final_gain).astype(bf16)
    every_rows = lax.all_gather(final, (TASK, TENSOR, DP), axis=0, tiled=True)

    def order(values):
        return jnp.transpose(
            values.reshape(tasks, halves, tensors, span_rows), (0, 2, 1, 3)
        ).reshape(-1)

    ordered_targets, ordered_mask = order(targets), order(loss_mask)
    logits = lax.dot_general(
        every_rows, unembedding, (((1,), (1,)), ((), ())), preferred_element_type=f32
    )
    capped = LOGIT_CAP * jnp.tanh(logits / LOGIT_CAP)
    vocab_ids = lax.axis_index((TASK, TENSOR, DP)) * unembedding.shape[0] + jnp.arange(
        unembedding.shape[0], dtype=jnp.int32
    )
    local_sumexp = jnp.sum(jnp.exp(capped), axis=1)
    local_target = jnp.sum(
        jnp.where(ordered_targets[:, None] == vocab_ids[None, :], capped, 0.0), axis=1
    )
    both = jnp.stack([local_sumexp, local_target])
    both = total_over_group(total_over(both, TENSOR))
    sumexp, target_logit = both[0], both[1]
    counted = ordered_mask.astype(f32)
    losses = (jnp.log(sumexp) - target_logit) * counted
    summary = jnp.stack([jnp.sum(losses), jnp.sum(counted)])
    losses = jnp.transpose(
        losses.reshape(tasks, tensors, halves, span_rows), (0, 2, 1, 3)
    ).reshape(-1)
    own_losses = lax.dynamic_slice_in_dim(losses, group_index * row_count, row_count, 0)
    return (own_losses, summary)


def paired(blocks):
    return blocks + [swap(block, TASK, 1) for block in blocks]


def send_hidden(hidden, kept, tensor):
    tensors = lax.axis_size(TENSOR)
    rows = hidden.shape[0] // tensors
    cut = hidden.shape[0] // 2
    hidden = after([hidden], [kept])[0]
    side = tensor // (tensors // 2)
    share = lax.dynamic_slice_in_dim(hidden, tensor * rows, rows, 0)
    mine = lax.dynamic_slice_in_dim(hidden, side * cut, cut, 0)
    rest = lax.dynamic_slice_in_dim(hidden, (1 - side) * cut, cut, 0)
    dp_mine = swap(mine, DP, 1)
    by_task = swap(share, TASK, 2)
    dp_rest = swap(rest, DP, 1)
    both_mine = swap(dp_mine, TASK, 2)
    shares = [by_task] + [swap(by_task, TENSOR, m) for m in range(1, tensors)]
    both_rest = []
    for m in range(tensors // 2, tensors):
        if m % 2:
            start = ((tensor ^ m) % (tensors // 2)) * rows
            block = lax.dynamic_slice_in_dim(dp_rest, start, rows, 0)
            both_rest.append(swap(block, TASK, 2))
        else:
            both_rest.append(swap(shares[m], DP, 1))
    return [hidden, dp_mine, dp_rest], [both_mine], shares + both_rest


def split_tail(
    where,
    attention,
    piece_out,
    inverse_gains,
    late_rows,
    base,
    hidden,
    unembedding,
    targets,
    loss_mask,
):
    bf16, f32 = jnp.bfloat16, jnp.float32
    tasks = lax.axis_size(TASK)
    tensors = lax.axis_size(TENSOR)
    halves = lax.axis_size(DP)
    row_count, width = hidden.shape
    out_rows, _ = piece_out.shape
    groups = tasks * halves
    vocab = unembedding.shape[0]
    place = where
    to_plain, to_post = inverse_gains

    features = tensors * tasks * out_rows
    received = after([swap(attention, TENSOR, m) for m in range(1, tensors)], base[1:])
    heads = kernel_call(
        functools.partial(heads_body, list(range(tensors))),
        [place, attention] + received,
        [SMEM] + [VMEM] * tensors,
        [shape_of((row_count, features), bf16)],
    )[0]
    late = contract(paired(after(late_rows, [attention])), unembedding, f32)
    shares = after([swap(piece_out, TENSOR, m) for m in range(1, tensors)], [attention])
    column = jnp.concatenate([piece_out] + shares, axis=0)
    by_task, by_dp = swap(column, TASK, 2), swap(column, DP, 1)
    cut = column.shape[0] // 2
    parts = [
        (0, 0, 0, column),
        (2, 0, 0, by_task),
        (0, 1, 0, by_dp),
        (2, 1, 0, swap(by_dp[:cut], TASK, 2)),
        (2, 1, cut // out_rows, swap(by_task[cut:], DP, 1)),
    ]
    parts += [(tm ^ 1, dm, first, swap(b, TASK, 1)) for tm, dm, first, b in parts]
    tied = after([part[3] for part in parts[3:5]], [late])
    parts[3:5] = [part[:3] + (block,) for part, block in zip(parts[3:5], tied)]
    plain = kernel_call(
        functools.partial(assemble_body, [part[:3] for part in parts]),
        [place] + [part[3] for part in parts],
        [SMEM] + [VMEM] * len(parts),
        [shape_of((tensors, tasks, out_rows, width), bf16)],
    )[0]
    plain = plain.reshape(features, width)
    mixed = contract([plain], unembedding, bf16)

    stats = kernel_call(
        statistics_body,
        [heads, plain, hidden, to_plain, to_post],
        [VMEM] * 5,
        [shape_of((8, row_count), f32)],
        flops=2 * row_count * features * width,
    )[0]
    every_heads = gather_group(heads)
    every_stats = gather_group(stats)
    both = kernel_call(
        functools.partial(score_body, [(tm, dm) for tm, dm, _ in every_heads], halves, tensors),
        [where, targets.reshape(groups, row_count), mixed]
        + [b for _, _, b in every_heads]
        + [b for _, _, b in every_stats]
        + base + [late],
        [SMEM] + [VMEM] * (5 + 2 * groups),
        [shape_of((2, groups, row_count), f32)],
        flops=2 * groups * row_count * features * vocab,
        transcendentals=2 * groups * row_count * vocab,
    )[0]
    both = total_over(both, TENSOR)
    parts = [swap_two(both, tm, dm) for tm in range(0, tasks, 2) for dm in range(halves) if tm or dm]
    for part in parts:
        both = both + part
    own, summary = pl.pallas_call(
        functools.partial(loss_body, halves),
        out_shape=[shape_of((1, row_count), f32), shape_of((2,), f32)],
        in_specs=[SMEM] + [VMEM] * 3,
        out_specs=[VMEM, SMEM],
        name="loss",
    )(place, loss_mask.reshape(groups, row_count), both, swap(both, TASK, 1))
    return own.reshape(row_count), summary


def on_device(
    hidden,
    pre_gain,
    base_query,
    base_keyval,
    base_output,
    delta_query,
    delta_keyval,
    delta_output,
    trim_query,
    trim_keyval,
    trim_output,
    sign_query,
    sign_keyval,
    sign_output,
    post_gain,
    final_gain,
    unembedding,
    targets,
    loss_mask,
):
    bf16, f32 = jnp.bfloat16, jnp.float32
    tasks = lax.axis_size(TASK)
    tensors = lax.axis_size(TENSOR)
    halves = lax.axis_size(DP)
    task, dp, tensor = lax.axis_index(TASK), lax.axis_index(DP), lax.axis_index(TENSOR)
    place = jnp.stack([task, dp, tensor]).astype(jnp.int32)
    row_count, width = hidden.shape
    half = base_query.shape[0]
    quarter = half // tasks
    out_rows = base_output.shape[0] // tasks

    kept_in = kernel_call(
        functools.partial(trim_input_body, tasks),
        [
            place,
            jnp.swapaxes(trim_query, 1, 2),
            jnp.swapaxes(trim_keyval, 2, 3),
            sign_query.T,
            jnp.swapaxes(sign_keyval, 1, 2),
            delta_query,
            jnp.swapaxes(delta_keyval, 2, 3),
        ],
        [SMEM] * 5 + [VMEM] * 2,
        [shape_of((quarter, 2 * LANES), bf16)] * tasks,
        [pltpu.VMEM((half, LANES), f32)],
        grant=56 * 2**20,
    )
    got_in = [kept_in[0]] + [swap(kept_in[j], TASK, j) for j in range(1, tasks)]
    kept_out = kernel_call(
        functools.partial(trim_output_body, tasks),
        [place, trim_output, sign_output, delta_output],
        [SMEM] * 3 + [VMEM],
        [shape_of((out_rows, half), bf16)] * tasks,
    )
    base_in = kernel_call(
        base_input_body,
        [place, base_query, jnp.swapaxes(base_keyval, 1, 2)],
        [SMEM] + [VMEM] * 2,
        [shape_of((quarter, 2 * LANES), bf16)],
        [pltpu.VMEM((half, LANES), f32)],
    )[0]

    early_hidden = after([hidden], [kept_in[0]])[0]
    blocks = width // quarter
    normed, scaled = kernel_call(
        prepare_body,
        [early_hidden, pre_gain[None, :], final_gain[None, :]],
        [VMEM] * 3,
        [shape_of((blocks, row_count, quarter), bf16), shape_of((row_count, width), bf16)],
    )
    early_place = after([place], [scaled])[0]
    group_index = early_place[0] * halves + early_place[1]
    query_positions = group_index * row_count + jnp.arange(row_count, dtype=jnp.int32)
    half_head = LANES // 2
    frequencies = jnp.exp(
        -jnp.log(ROPE_BASE) * 2.0 * jnp.arange(half_head, dtype=jnp.int32).astype(f32) / LANES
    )
    angles = query_positions.astype(f32)[:, None] * frequencies[None, :]
    cosine, sine = jnp.cos(angles), jnp.sin(angles)
    cosine = jnp.concatenate([cosine, cosine], axis=1)
    sine = jnp.concatenate([-sine, sine], axis=1)

    gathered_bytes = tensors * base_output.shape[0] * width * base_output.dtype.itemsize
    low_rank = gathered_bytes <= 6 * 2**20 and tensors in (2, 4)
    where = jnp.concatenate(
        [place, (lax.axis_index((TASK, TENSOR, DP)) * unembedding.shape[0]).astype(jnp.int32)[None]]
    )

    def row_table(post, last):
        if not low_rank:
            return [jnp.ones((1, width), f32), where]
        both = (post * last)[None, :]
        return [both, 1.0 / both, (1.0 / last)[None, :], where]

    gains = after([post_gain, final_gain], [scaled])
    rows = row_table(*gains)
    weight_gain, where = rows[0], rows[-1]
    piece_in = kernel_call(
        merge_input_body,
        [base_in] + got_in,
        [VMEM] * (1 + tasks),
        [shape_of((quarter, 2 * LANES), bf16)],
    )[0]
    pieces_in = gather_group(piece_in)
    masks = [(tm, dm) for tm, dm, _ in pieces_in]

    kept_out = after(kept_out, [piece_in])
    got_out = [kept_out[0]] + [swap(kept_out[j], TASK, j) for j in range(1, tasks)]
    got_out = after(got_out, [b for _, _, b in pieces_in[1:4]])
    if low_rank:
        early_rows, middle_rows, late_rows = send_hidden(scaled, kept_in[0], tensor)
        early_rows[:1] = after(early_rows[:1], [cosine, sine] + list(rows))
        base = [contract(paired(early_rows[:1]), unembedding, f32)]
        base.append(contract(paired(early_rows[1:]), unembedding, f32))
    piece_out = kernel_call(
        merge_output_body,
        [place, weight_gain, base_output] + got_out,
        [SMEM] + [VMEM] * (2 + tasks),
        [shape_of((out_rows, half), bf16)],
    )[0]

    queries, keyval = kernel_call(
        functools.partial(project_body, masks, tasks),
        [place, normed, cosine, sine] + [b for _, _, b in pieces_in],
        [SMEM] + [VMEM] * (3 + len(masks)),
        [shape_of((row_count, LANES), bf16)] * 2,
        flops=2 * row_count * width * 2 * LANES,
    )
    other = swap(keyval, TENSOR, 1)
    joined = kernel_call(
        join_body,
        [place, cosine, sine, keyval, other],
        [SMEM] + [VMEM] * 4,
        [shape_of((row_count, 2 * LANES), bf16)],
    )[0]
    every_keyval = gather_group(joined)
    attention = kernel_call(
        functools.partial(attend_body, masks, halves),
        [place, queries] + [b for _, _, b in every_keyval],
        [SMEM] + [VMEM] * (1 + len(masks)),
        [shape_of((row_count, LANES), bf16)],
        flops=4 * row_count * row_count * LANES * len(masks),
        transcendentals=2 * row_count * row_count * len(masks),
    )[0]
    if not low_rank:
        return general_tail(
            place, masks, attention, piece_out, hidden, post_gain, final_gain, unembedding, targets, loss_mask
        )
    return split_tail(
        where,
        attention,
        piece_out,
        rows[1:3],
        middle_rows + late_rows,
        base,
        hidden,
        unembedding,
        targets,
        loss_mask,
    )


def solution(mesh):
    return jax.shard_map(
        on_device,
        mesh=mesh,
        in_specs=(
            P((TASK, DP), None),
            P(),
            P(DP, TENSOR),
            P(None, DP, TENSOR),
            P(TENSOR, DP),
            P(TASK, DP, TENSOR),
            P(TASK, None, DP, TENSOR),
            P(TASK, TENSOR, DP),
            P(TASK, DP, TENSOR),
            P(TASK, None, DP, TENSOR),
            P(TASK, TENSOR, DP),
            P(DP, TENSOR),
            P(None, DP, TENSOR),
            P(TENSOR, DP),
            P(),
            P(),
            P((TASK, TENSOR, DP), None),
            P(),
            P(),
        ),
        out_specs=(P((TASK, DP)), P()),
        check_vma=False,
    )
```
